256 devices in a mesh: aa: 8 (over x, core), ba: 32 (over z, y).
Axes of the slice: x: 4, y: 4, z: 8, core: 2. Of those that a mesh axis runs over, the one named last changes fastest.
Arguments:
- spec_in: bfloat16 [640, 2, 3, 32, 1288], P('aa', None, None, 'ba'), may hold values from -0.23925781 to 0.23925781
- legendre: bfloat16 [640, 32, 1288], P('aa'), may hold values from -0.15625 to 0.15625
- pair_wave: int32 [640], replicated, may hold values from 0 to 639, each once
- quad_weight: float32 [32], replicated, may hold values from 1 to 3
- forcing: bfloat16 [64, 3, 32, 5248], P('aa', None, None, 'ba'), may hold values from -6 to 6
Outputs:
- grid: bfloat16 [64, 3, 32, 5248], P('aa', None, None, 'ba')
- spec_out: bfloat16 [640, 2, 3, 32, 1288], P('aa', None, None, 'ba')
The draws below stay inside these ranges and needn't reach their ends.
Inputs may be any that keep to these rules, and one draw needn't show every extreme that they name: Each value appears once; pair p holds the zonal wavenumbers pair_wave[p] and 1279 - pair_wave[p].
All inputs are finite; a program needn't handle non-finite values.
Results may differ from the reference program's by a relative error of at most 0.012.
Values may be sent and summed in bfloat16 or wider, within the bound.
No kernel may reach another device: no remote copies, remote signals or barrier semaphores. Data moves between devices by JAX's collectives and lax.ppermute only.
A program may use at most 128 MiB of HBM per device.

```python
import math
import jax
import jax.numpy as jnp
from jax import lax

TRUNCATION = 1279
FIELDS = 3
WAVE_PAIRS = 640
PAIR_SLOTS = 1288
KEPT_LATS = 32
GRID_ROWS = 64
LON_PAD = 5248
LEVELS = 32


def levels(own_key, shape, shards, smallest, high):
    def one(position, shards_of):
        steps = jax.random.uniform(jax.random.fold_in(jax.random.fold_in(own_key, 6), position), (shards_of,), jnp.float32, smallest / len(shards), high / len(shards))
        return jnp.repeat(jnp.exp(steps), shape[position] // shards_of).reshape((-1,) + (1,) * (len(shape) - position - 1))

    level = one(*shards[0])
    for cut in shards[1:]:
        level = level * one(*cut)
    return level


def normal_values(rng, shape, scale, most, cuts=(), kind=jnp.bfloat16):
    drawn = jax.random.normal(rng, shape, jnp.float32) * scale
    if len(cuts) > 0:
        drawn = levels(rng, shape, cuts, -0.22, 0.18) * drawn
    return jnp.clip(drawn, min=-most, max=most).astype(kind)


def setup_inputs(seed: int = 0) -> dict:
    keys = jax.random.split(jax.random.key(seed), 6)
    spec_in = normal_values(keys[0], (WAVE_PAIRS, 2, FIELDS, LEVELS, PAIR_SLOTS), 0.04, 0.23925781, ((0, 8), (3, 32)))
    legendre = normal_values(keys[1], (WAVE_PAIRS, KEPT_LATS, PAIR_SLOTS), (TRUNCATION + 1) ** -0.5, 0.15625, ((0, 8),))
    pair_wave = jax.random.permutation(keys[2], WAVE_PAIRS).astype(jnp.int32)
    quad_weight = jnp.clip(jax.random.uniform(keys[3], (KEPT_LATS,), jnp.float32, 1.0, 3.0), 1.0, 3.0)
    forcing = normal_values(keys[4], (GRID_ROWS, FIELDS, LEVELS, LON_PAD), 1.0, 6.0, ((0, 8), (3, 32)))
    return dict(spec_in=spec_in, legendre=legendre, pair_wave=pair_wave, quad_weight=quad_weight, forcing=forcing)


def slot_masks(first_waves, slot_count):
    slots = jnp.arange(slot_count, dtype=jnp.int32)[None, :]
    limit = TRUNCATION - first_waves.astype(jnp.int32)[:, None]
    own_first = (slots <= limit).astype(jnp.float32)
    own_second = ((slots > limit) & (slots <= TRUNCATION + 1)).astype(jnp.float32)
    sign_first = (1 - 2 * (slots % 2)).astype(jnp.float32)
    sign_second = (1 - 2 * ((slots - 1 - limit) % 2)).astype(jnp.float32)
    north = jnp.stack([own_first, own_second], axis=1)
    south = jnp.stack([own_first * sign_first, own_second * sign_second], axis=1)
    return jnp.stack([north, south], axis=1)

def inverse_pair(operands):
    table, coeffs, masking = operands
    return jnp.einsum('ts,hws,rfls->thwrfl', table.astype(jnp.float32), masking, coeffs.astype(jnp.float32)).astype(jnp.bfloat16)

def direct_pair(operands):
    table, parts, masking = operands
    return jnp.einsum('ts,hws,thwrfl->rfls', table.astype(jnp.float32), masking, parts.astype(jnp.float32)).astype(jnp.bfloat16)

def reference(spec_in, legendre, pair_wave, quad_weight, forcing):
    masking = slot_masks(pair_wave, PAIR_SLOTS)
    fourier = lax.map(inverse_pair, (legendre, spec_in, masking))
    wavenumbers = jnp.stack([pair_wave, TRUNCATION - pair_wave], axis=1).astype(jnp.int32)
    flat_waves = wavenumbers.reshape(-1)
    doubling = jnp.where(wavenumbers == 0, 1.0, 2.0).astype(jnp.float32)
    grid_rows = []
    for latitude in range(KEPT_LATS):
        length = 20 + 4 * (TRUNCATION + 1 - KEPT_LATS + latitude)
        for hemisphere in range(2):
            values = fourier[:, latitude, hemisphere].astype(jnp.float32)
            real_part = values[:, :, 0] * doubling[:, :, None, None]
            imag_part = values[:, :, 1] * doubling[:, :, None, None]
            spectrum_real = jnp.zeros((length, FIELDS, LEVELS), jnp.float32).at[flat_waves].set(real_part.reshape(-1, FIELDS, LEVELS))
            spectrum_imag = jnp.zeros((length, FIELDS, LEVELS), jnp.float32).at[flat_waves].set(imag_part.reshape(-1, FIELDS, LEVELS))
            spectrum = lax.complex(spectrum_real, spectrum_imag)
            row_values = jnp.real(jnp.fft.ifft(spectrum, axis=0)) * length
            row_values = jnp.pad(row_values, ((0, LON_PAD - length), (0, 0), (0, 0)))
            grid_rows.append(jnp.transpose(row_values, (1, 2, 0)))
    grid = jnp.stack(grid_rows).astype(jnp.bfloat16)
    grid_wide = grid.astype(jnp.float32)
    tendency = (grid_wide * jnp.roll(grid_wide, -1, axis=1) + forcing.astype(jnp.float32)).astype(jnp.bfloat16)
    direct_lats = []
    for latitude in range(KEPT_LATS):
        length = 20 + 4 * (TRUNCATION + 1 - KEPT_LATS + latitude)
        factor = quad_weight[latitude] / math.sqrt(length)
        halves = []
        for hemisphere in range(2):
            samples = tendency[2 * latitude + hemisphere, :, :, :length].astype(jnp.float32)
            spectrum = jnp.fft.fft(samples, axis=-1)
            picked = spectrum[:, :, flat_waves].reshape(FIELDS, LEVELS, WAVE_PAIRS, 2)
            combined = jnp.stack([jnp.real(picked) * factor, jnp.imag(picked) * factor])
            halves.append(jnp.transpose(combined, (3, 4, 0, 1, 2)))
        direct_lats.append(jnp.stack(halves, axis=1))
    direct = jnp.stack(direct_lats, axis=1).astype(jnp.bfloat16)
    spec_out = lax.map(direct_pair, (legendre, direct, masking))
    return (grid, spec_out)
```

```python
import functools
import math

import jax
import jax.numpy as jnp
from jax import lax
from jax.experimental import pallas as pl
from jax.experimental.pallas import tpu as pltpu
from jax.sharding import PartitionSpec as P

TRUNCATION = 1279
FIELDS = 3
PAIRS = 80
WAVES = 1280
COLS = 164
OWNERS = 32
BROWS = 176
PAIR_BLOCK = 8
F32 = jnp.float32
BF16 = jnp.bfloat16
NT = (((1,), (1,)), ((), ()))
NN = (((1,), (0,)), ((), ()))


def vmem_params(mib):
    return pltpu.CompilerParams(vmem_limit_bytes=mib << 20)


def swap_kernel(x_ref, o_ref, left, right):
    major, minor = x_ref.shape[0], x_ref.shape[1]
    x = x_ref[...].astype(F32)
    left[...] = x[:, :, :128].reshape(major * minor, 128)
    right[:, 0:36] = x[:, :, 128:164].reshape(major * minor, 36)
    for k in range(minor):
        o_ref[k, :, 0:128] = left[pl.ds(k, major, stride=minor), :].astype(BF16)
        o_ref[k, :, 128:164] = right[pl.ds(k, major, stride=minor), :][:, 0:36].astype(BF16)


def swap_leading(x):
    major, minor, cols = x.shape
    return pl.pallas_call(
        swap_kernel,
        out_shape=jax.ShapeDtypeStruct((minor, major, cols), BF16),
        scratch_shapes=[pltpu.VMEM((major * minor, 128), F32), pltpu.VMEM((major * minor, 128), F32)],
        compiler_params=vmem_params(16),
        cost_estimate=pl.CostEstimate(flops=0, bytes_accessed=4 * major * minor * 256, transcendentals=0),
        name="swap_leading",
    )(x)


def legendre_inverse_kernel(pw_ref, me_ref, leg_ref, spec_ref, out_ref, by_pair, by_lat):
    step = pl.program_id(0)
    slots = leg_ref.shape[2]
    slot = lax.broadcasted_iota(jnp.int32, (8, slots), 1)
    alternate = jnp.where(slot % 2 == 0, 1.0, -1.0).astype(F32)
    valid = slot <= TRUNCATION + 1
    row = lax.broadcasted_iota(jnp.int32, (32, 32), 0)
    for k in range(PAIR_BLOCK):
        pair = step * PAIR_BLOCK + k
        wave = pw_ref[me_ref[0] * PAIRS + pair]
        first = slot <= TRUNCATION - wave
        a = jnp.where(valid, spec_ref[k].astype(F32), 0.0)
        b = a * alternate
        lhs = jnp.concatenate(
            [
                jnp.where(first, a, 0.0),
                jnp.where(first, b, 0.0),
                jnp.where(first, 0.0, a),
                jnp.where(first, 0.0, b),
            ],
            axis=0,
        ).astype(BF16)
        sums = lax.dot_general(lhs, leg_ref[k], NT, preferred_element_type=F32)
        sign = (1 - 2 * (wave % 2)).astype(F32)
        sums = jnp.where(row >= 24, sums * sign, sums)
        by_pair[pl.ds(pair, 32, stride=PAIRS), :] = jnp.concatenate(
            [sums, jnp.zeros((32, 96), F32)], axis=1
        )

    @pl.when(step == pl.num_programs(0) - 1)
    def _():
        for half in range(4):
            h, w = half % 2, half // 2
            for c in range(6):
                start = (half * 8 + c) * PAIRS
                turned = jnp.concatenate(
                    [by_pair[start : start + PAIRS, :], jnp.zeros((48, 128), F32)], axis=0
                ).T
                by_lat[w, pl.ds(h * 6 + c, 32, stride=12), :] = turned[0:32, :]
        x, core = me_ref[0] // 2, me_ref[0] % 2
        for s in range(4):
            for d in range(2):
                dest = ((x + s) % 4) * 2 + (core + d) % 2
                rows = pl.ds(pl.multiple_of(dest * 48, 8), 48)
                out_ref[s, d, :, 0:128] = by_lat[0, rows, :].astype(BF16)
                out_ref[s, d, :, 128:256] = by_lat[1, rows, :].astype(BF16)


def legendre_inverse(pair_wave, me, legendre, spec):
    slots = legendre.shape[2]
    return pl.pallas_call(
        legendre_inverse_kernel,
        grid_spec=pltpu.PrefetchScalarGridSpec(
            num_scalar_prefetch=2,
            grid=(PAIRS // PAIR_BLOCK,),
            in_specs=[
                pl.BlockSpec((PAIR_BLOCK, 32, slots), lambda i, *_: (i, 0, 0)),
                pl.BlockSpec((PAIR_BLOCK, 8, slots), lambda i, *_: (i, 0, 0)),
            ],
            out_specs=pl.BlockSpec((4, 2, 48, 256), lambda i, *_: (0, 0, 0, 0)),
            scratch_shapes=[pltpu.VMEM((32 * PAIRS, 128), F32), pltpu.VMEM((2, 384, 128), F32)],
        ),
        out_shape=jax.ShapeDtypeStruct((4, 2, 48, 256), BF16),
        compiler_params=vmem_params(32),
        cost_estimate=pl.CostEstimate(flops=2 * 80 * 32 * 32 * 1288, bytes_accessed=9_000_000, transcendentals=0),
        name="legendre_inverse",
    )(pair_wave, me, legendre, spec)


def join_pieces(pieces):
    lane = lax.broadcasted_iota(jnp.int32, pieces[0].shape, 1)
    rolled = [pltpu.roll(p, (80 * i) % 128, axis=1) if (80 * i) % 128 else p for i, p in enumerate(pieces)]
    tiles = []
    for k in range(10):
        tile = None
        for i in range(16):
            low, high = 80 * i - 128 * k, 80 * i + 80 - 128 * k
            if high <= 0 or low >= 128:
                continue
            tile = rolled[i] if tile is None else jnp.where(lane >= low, rolled[i], tile)
        tiles.append(tile)
    return tiles


def cut_piece(ref, i):
    tile, shift = (80 * i) // 128, (80 * i) % 128
    low = ref[:, tile * 128 : tile * 128 + 128]
    if shift == 0:
        return low
    low = pltpu.roll(low, 128 - shift, axis=1)
    if shift + 80 <= 128:
        return low
    high = pltpu.roll(ref[:, tile * 128 + 128 : tile * 128 + 256], 128 - shift, axis=1)
    lane = lax.broadcasted_iota(jnp.int32, low.shape, 1)
    return jnp.where(lane < 128 - shift, low, high)


def cos_sin(turn, length):
    times = jnp.floor(turn * (1.0 / length) + 0.5)
    u = (turn - times * length) * (math.pi / length)
    u2 = u * u
    s = u * (
        1.0
        + u2
        * (
            -1.0 / 6
            + u2 * (1.0 / 120 + u2 * (-1.0 / 5040 + u2 * (1.0 / 362880 + u2 * (-1.0 / 39916800))))
        )
    )
    c = 1.0 + u2 * (
        -0.5
        + u2
        * (
            1.0 / 24
            + u2
            * (-1.0 / 720 + u2 * (1.0 / 40320 + u2 * (-1.0 / 3628800 + u2 * (1.0 / 479001600))))
        )
    )
    return 1.0 - 2.0 * s * s, 2.0 * s * c


def table_kernel(me_ref, waves_ref, outer_ref, inner_ref, factor_ref, wave_row):
    lat = pl.program_id(0)
    me = me_ref[0]
    x, core = me // 2, me % 2

    @pl.when(lat == 0)
    def _():
        pieces = []
        for d in range(2):
            for s in range(4):
                source = ((x + 4 - s) % 4) * 2 + (core + d) % 2
                for w in range(2):
                    pieces.append(jnp.broadcast_to(waves_ref[source, w : w + 1, :], (8, 128)))
        for k, tile in enumerate(join_pieces(pieces)):
            wave_row[:, 128 * k : 128 * k + 128] = tile
            factor_ref[:, 128 * k : 128 * k + 128] = jnp.where(tile == 0.0, 1.0, 2.0)

    length = (5012 + 16 * me + 4 * lat).astype(F32)
    length = jnp.full((8, WAVES), length, F32)
    wave = wave_row[...]
    eight = lax.broadcasted_iota(jnp.int32, (8, WAVES), 0).astype(F32)
    low_c, low_s = cos_sin(wave * (eight * COLS), length)
    high_c, high_s = cos_sin(wave * (eight * (8 * COLS)), length)
    for k in range(4):
        hc, hs = high_c[k : k + 1, :], high_s[k : k + 1, :]
        outer_ref[0, 0, 8 * k : 8 * k + 8, :] = low_c * hc - low_s * hs
        outer_ref[0, 1, 8 * k : 8 * k + 8, :] = low_s * hc + low_c * hs
    low_c, low_s = cos_sin(wave * eight, length)
    for block in range(3):
        high_c, high_s = cos_sin(wave * (eight * 8.0 + 64.0 * block), length)
        for k in range(0, 8, 2):
            base = 64 * block + 8 * k
            if base >= BROWS:
                continue
            parts_c, parts_s = [], []
            for kk in (k, k + 1):
                hc, hs = high_c[kk : kk + 1, :], high_s[kk : kk + 1, :]
                parts_c.append(low_c * hc - low_s * hs)
                parts_s.append(low_s * hc + low_c * hs)
            inner_ref[0, base : base + 16, 0:WAVES] = jnp.concatenate(parts_c, axis=0).astype(BF16)
            inner_ref[0, base : base + 16, WAVES:] = jnp.concatenate(parts_s, axis=0).astype(BF16)


def phase_tables(me, waves):
    return pl.pallas_call(
        table_kernel,
        grid_spec=pltpu.PrefetchScalarGridSpec(
            num_scalar_prefetch=1,
            grid=(4,),
            in_specs=[pl.BlockSpec((8, 2, 128), lambda i, *_: (0, 0, 0))],
            out_specs=[
                pl.BlockSpec((1, 2, OWNERS, WAVES), lambda i, *_: (i, 0, 0, 0)),
                pl.BlockSpec((1, BROWS, 2 * WAVES), lambda i, *_: (i, 0, 0)),
                pl.BlockSpec((8, WAVES), lambda i, *_: (0, 0)),
            ],
            scratch_shapes=[pltpu.VMEM((8, WAVES), F32)],
        ),
        out_shape=[
            jax.ShapeDtypeStruct((4, 2, OWNERS, WAVES), F32),
            jax.ShapeDtypeStruct((4, BROWS, 2 * WAVES), BF16),
            jax.ShapeDtypeStruct((8, WAVES), F32),
        ],
        compiler_params=vmem_params(24),
        cost_estimate=pl.CostEstimate(flops=40_000_000, bytes_accessed=5_000_000, transcendentals=0),
        name="phase_tables",
    )(me, waves)


def inside_mask(me, lat):
    length = 5012 + 16 * me + 4 * lat
    owner = lax.broadcasted_iota(jnp.int32, (OWNERS, BROWS), 0)
    col = lax.broadcasted_iota(jnp.int32, (OWNERS, BROWS), 1)
    return (col < COLS) & (owner * COLS + col < length)


def inverse_kernel(
    me_ref, kept_ref, got_ref, outer_ref, inner_ref, factor_ref, grid_ref, send_ref, coeffs, turned, left, right
):
    lat = pl.program_id(0)

    @pl.when(lat == 0)
    def _():
        pieces = []
        for ref in (kept_ref, got_ref):
            for s in range(4):
                for w in range(2):
                    pieces.append(ref[s, :, 128 * w : 128 * w + 128].astype(F32))
        for k, tile in enumerate(join_pieces(pieces)):
            coeffs[:, 128 * k : 128 * k + 128] = tile * factor_ref[0:1, 128 * k : 128 * k + 128]

    for r in range(6):
        h, f = r // 3, r % 3
        real = coeffs[pl.ds(lat * 12 + h * 6 + f, 1), :]
        imag = coeffs[pl.ds(lat * 12 + h * 6 + 3 + f, 1), :]
        oc, os = outer_ref[0, 0], outer_ref[0, 1]
        turned[32 * r : 32 * r + 32, 0:WAVES] = (real * oc - imag * os).astype(BF16)
        turned[32 * r : 32 * r + 32, WAVES:] = (-(real * os + imag * oc)).astype(BF16)
    rows = lax.dot_general(turned[...], inner_ref[0], NT, preferred_element_type=F32)
    inside = inside_mask(me_ref[0], lat)
    for r in range(6):
        value = jnp.where(inside, rows[32 * r : 32 * r + 32, :], 0.0)
        grid_ref[0, 32 * r : 32 * r + 32, :] = value.astype(BF16)
        left[pl.ds(lat * 6 + r, 32, stride=24), :] = value[:, 0:128]
        right[pl.ds(lat * 6 + r, 32, stride=24), :] = jnp.concatenate(
            [value[:, 128:BROWS], jnp.zeros((OWNERS, 256 - BROWS), F32)], axis=1
        )

    @pl.when(lat == 3)
    def _():
        for j in range(OWNERS):
            send_ref[j, :, 0:128] = left[24 * j : 24 * j + 24, :].astype(BF16)
            send_ref[j, :, 128:COLS] = right[24 * j : 24 * j + 24, 0:36].astype(BF16)


def inverse_rows(me, kept, got, outer, inner, factor):
    return pl.pallas_call(
        inverse_kernel,
        grid_spec=pltpu.PrefetchScalarGridSpec(
            num_scalar_prefetch=1,
            grid=(4,),
            in_specs=[
                pl.BlockSpec((4, 48, 256), lambda i, *_: (0, 0, 0)),
                pl.BlockSpec((4, 48, 256), lambda i, *_: (0, 0, 0)),
                pl.BlockSpec((1, 2, OWNERS, WAVES), lambda i, *_: (i, 0, 0, 0)),
                pl.BlockSpec((1, BROWS, 2 * WAVES), lambda i, *_: (i, 0, 0)),
                pl.BlockSpec((8, WAVES), lambda i, *_: (0, 0)),
            ],
            out_specs=[
                pl.BlockSpec((1, 192, BROWS), lambda i, *_: (i, 0, 0)),
                pl.BlockSpec((OWNERS, 24, COLS), lambda i, *_: (0, 0, 0)),
            ],
            scratch_shapes=[
                pltpu.VMEM((48, WAVES), F32),
                pltpu.VMEM((192, 2 * WAVES), BF16),
                pltpu.VMEM((768, 128), F32),
                pltpu.VMEM((768, 128), F32),
            ],
        ),
        out_shape=[
            jax.ShapeDtypeStruct((4, 192, BROWS), BF16),
            jax.ShapeDtypeStruct((OWNERS, 24, COLS), BF16),
        ],
        compiler_params=vmem_params(32),
        cost_estimate=pl.CostEstimate(flops=700_000_000, bytes_accessed=6_000_000, transcendentals=0),
        name="inverse_rows",
    )(me, kept, got, outer, inner, factor)


def direct_kernel(
    me_ref, weight_ref, forcing_ref, grid_ref, outer_ref, inner_ref, out_ref, left, right, samples, sums
):
    lat = pl.program_id(0)
    me = me_ref[0]

    @pl.when(lat == 0)
    def _():
        for j in range(OWNERS):
            left[24 * j : 24 * j + 24, :] = forcing_ref[j, :, 0:128].astype(F32)
            right[24 * j : 24 * j + 24, 0:36] = forcing_ref[j, :, 128:COLS].astype(F32)

    inside = inside_mask(me, lat)
    for r in range(6):
        h, f = r // 3, r % 3
        other = h * 3 + (f + 1) % 3
        product = grid_ref[0, 32 * r : 32 * r + 32, :].astype(F32) * grid_ref[
            0, 32 * other : 32 * other + 32, :
        ].astype(F32)
        force = jnp.concatenate(
            [
                left[pl.ds(lat * 6 + r, 32, stride=24), :],
                right[pl.ds(lat * 6 + r, 32, stride=24), :][:, 0 : BROWS - 128],
            ],
            axis=1,
        )
        samples[32 * r : 32 * r + 32, :] = jnp.where(inside, product + force, 0.0).astype(BF16)
    length = jnp.full((1, 256), (5012 + 16 * me + 4 * lat).astype(F32), F32)
    scale = weight_ref[me * 4 + lat] * lax.rsqrt(length)
    data = samples[...]
    for n in range(0, WAVES, 256):
        part_c = lax.dot_general(data, inner_ref[0, :, n : n + 256], NN, preferred_element_type=F32)
        part_s = lax.dot_general(
            data, inner_ref[0, :, WAVES + n : WAVES + n + 256], NN, preferred_element_type=F32
        )
        oc, os = outer_ref[0, 0, :, n : n + 256], outer_ref[0, 1, :, n : n + 256]
        for r in range(6):
            h, f = r // 3, r % 3
            pc, ps = part_c[32 * r : 32 * r + 32, :], part_s[32 * r : 32 * r + 32, :]
            real = jnp.sum(pc * oc - ps * os, axis=0, keepdims=True)
            imag = jnp.sum(ps * oc + pc * os, axis=0, keepdims=True)
            sums[pl.ds(lat * 12 + h * 6 + f, 1), n : n + 256] = real * scale
            sums[pl.ds(lat * 12 + h * 6 + 3 + f, 1), n : n + 256] = -imag * scale

    @pl.when(lat == 3)
    def _():
        for d in range(2):
            for s in range(4):
                for w in range(2):
                    piece = cut_piece(sums, (d * 4 + s) * 2 + w)
                    out_ref[s, d, :, 128 * w : 128 * w + 128] = piece.astype(BF16)


def direct_rows(me, weight, forcing, grid, outer, inner):
    return pl.pallas_call(
        direct_kernel,
        grid_spec=pltpu.PrefetchScalarGridSpec(
            num_scalar_prefetch=2,
            grid=(4,),
            in_specs=[
                pl.BlockSpec((OWNERS, 24, COLS), lambda i, *_: (0, 0, 0)),
                pl.BlockSpec((1, 192, BROWS), lambda i, *_: (i, 0, 0)),
                pl.BlockSpec((1, 2, OWNERS, WAVES), lambda i, *_: (i, 0, 0, 0)),
                pl.BlockSpec((1, BROWS, 2 * WAVES), lambda i, *_: (i, 0, 0)),
            ],
            out_specs=pl.BlockSpec((4, 2, 48, 256), lambda i, *_: (0, 0, 0, 0)),
            scratch_shapes=[
                pltpu.VMEM((768, 128), F32),
                pltpu.VMEM((768, 128), F32),
                pltpu.VMEM((192, BROWS), BF16),
                pltpu.VMEM((48, WAVES), F32),
            ],
        ),
        out_shape=jax.ShapeDtypeStruct((4, 2, 48, 256), BF16),
        compiler_params=vmem_params(32),
        cost_estimate=pl.CostEstimate(flops=700_000_000, bytes_accessed=6_000_000, transcendentals=0),
        name="direct_rows",
    )(me, weight, forcing, grid, outer, inner)


def legendre_direct_kernel(pw_ref, me_ref, kept_ref, got_ref, leg_ref, out_ref, by_lat, by_pair):
    step = pl.program_id(0)
    slots = leg_ref.shape[2]

    @pl.when(step == 0)
    def _():
        x, core = me_ref[0] // 2, me_ref[0] % 2
        for d, ref in enumerate((kept_ref, got_ref)):
            for s in range(4):
                source = ((x + s) % 4) * 2 + (core + d) % 2
                rows = pl.ds(pl.multiple_of(source * 48, 8), 48)
                for w in range(2):
                    by_lat[w, rows, :] = ref[s, :, 128 * w : 128 * w + 128].astype(F32)
        for w in range(2):
            for c in range(6):
                north = by_lat[w, pl.ds(c, 32, stride=12), :]
                south = by_lat[w, pl.ds(6 + c, 32, stride=12), :]
                for odd, value in enumerate((north + south, north - south)):
                    turned = jnp.concatenate([value, jnp.zeros((96, 128), F32)], axis=0).T
                    by_pair[pl.ds((w * 2 + odd) * 8 + c, PAIRS, stride=32), :] = turned[0:PAIRS, :]

    slot = lax.broadcasted_iota(jnp.int32, (8, slots), 1)
    even = slot % 2 == 0
    valid = slot <= TRUNCATION + 1
    for k in range(PAIR_BLOCK):
        pair = step * PAIR_BLOCK + k
        wave = pw_ref[me_ref[0] * PAIRS + pair]
        lhs = by_pair[pl.ds(pl.multiple_of(pair * 32, 32), 32), :][:, 0:32].astype(BF16)
        sums = lax.dot_general(lhs, leg_ref[k], NN, preferred_element_type=F32)
        first = jnp.where(even, sums[0:8], sums[8:16])
        second = jnp.where((slot + wave) % 2 == 0, sums[16:24], sums[24:32])
        value = jnp.where(slot <= TRUNCATION - wave, first, second)
        out_ref[k] = jnp.where(valid, value, 0.0)[0:6].astype(BF16)


def legendre_direct(pair_wave, me, kept, got, legendre):
    slots = legendre.shape[2]
    return pl.pallas_call(
        legendre_direct_kernel,
        grid_spec=pltpu.PrefetchScalarGridSpec(
            num_scalar_prefetch=2,
            grid=(PAIRS // PAIR_BLOCK,),
            in_specs=[
                pl.BlockSpec((4, 48, 256), lambda i, *_: (0, 0, 0)),
                pl.BlockSpec((4, 48, 256), lambda i, *_: (0, 0, 0)),
                pl.BlockSpec((PAIR_BLOCK, 32, slots), lambda i, *_: (i, 0, 0)),
            ],
            out_specs=pl.BlockSpec((PAIR_BLOCK, 6, slots), lambda i, *_: (i, 0, 0)),
            scratch_shapes=[pltpu.VMEM((2, 384, 128), F32), pltpu.VMEM((32 * PAIRS, 128), F32)],
        ),
        out_shape=jax.ShapeDtypeStruct((PAIRS, 6, slots), BF16),
        compiler_params=vmem_params(32),
        cost_estimate=pl.CostEstimate(flops=2 * 80 * 32 * 32 * 1288, bytes_accessed=9_000_000, transcendentals=0),
        name="legendre_direct",
    )(pair_wave, me, kept, got, legendre)


def exchange(parts, direction):
    came = [parts[0]]
    for s in range(1, 4):
        hop = [(i, ((i // 2 + direction * s) % 4) * 2 + i % 2) for i in range(8)]
        came.append(lax.ppermute(parts[s], "aa", hop))
    kept = jnp.stack([c[0] for c in came])
    passed = jnp.stack([c[1] for c in came])
    return kept, lax.ppermute(passed, "aa", [(i, i ^ 1) for i in range(8)])


def per_device(spec_in, legendre, pair_wave, quad_weight, forcing):
    me = lax.axis_index("aa").astype(jnp.int32).reshape(1)
    forcing_send = swap_leading(forcing.reshape(24, OWNERS, COLS))
    forcing_here = lax.all_to_all(forcing_send, "ba", split_axis=0, concat_axis=0, tiled=True)
    spec = jnp.pad(spec_in.reshape(PAIRS, 6, -1), ((0, 0), (0, 2), (0, 0)))
    fourier = legendre_inverse(pair_wave, me, legendre, spec)
    kept, got = exchange(fourier, 1)
    pairs = pair_wave.astype(F32).reshape(8, PAIRS)
    waves = jnp.pad(jnp.stack([pairs, TRUNCATION - pairs], axis=1), ((0, 0), (0, 0), (0, 48)))
    outer, inner, factor = phase_tables(me, waves)
    rows, grid_send = inverse_rows(me, kept, got, outer, inner, factor)
    grid_came = lax.all_to_all(grid_send, "ba", split_axis=0, concat_axis=0, tiled=True)
    direct = direct_rows(me, quad_weight, forcing_here, rows, outer, inner)
    kept, got = exchange(direct, -1)
    spec_out = legendre_direct(pair_wave, me, kept, got, legendre)
    grid = swap_leading(grid_came)
    return (
        grid.reshape(8, FIELDS, OWNERS, COLS),
        spec_out.reshape(PAIRS, 2, FIELDS, 1, -1),
    )


def solution(mesh):
    placed = (
        P("aa", None, None, "ba", None),
        P("aa", None, None),
        P(),
        P(),
        P("aa", None, None, "ba"),
    )
    return jax.shard_map(
        per_device,
        mesh=mesh,
        in_specs=placed,
        out_specs=(P("aa", None, None, "ba"), P("aa", None, None, "ba", None)),
        check_vma=False,
    )
```

```python
import functools
import math

import jax
import jax.numpy as jnp
from jax import lax
from jax.experimental import pallas as pl
from jax.experimental.pallas import tpu as pltpu
from jax.sharding import PartitionSpec as P

TRUNCATION = 1279
FIELDS = 3
PAIRS = 80
WAVES = 1280
COLS = 164
OWNERS = 32
BROWS = 176
TAIL = COLS - 128
PAIR_BLOCK = 16
F32 = jnp.float32
BF16 = jnp.bfloat16
NT = (((1,), (1,)), ((), ()))
NN = (((1,), (0,)), ((), ()))


def vmem_params(mib):
    return pltpu.CompilerParams(vmem_limit_bytes=mib << 20)


def join_tails(first, second, third):
    return first + pltpu.roll(second, TAIL, axis=1) + pltpu.roll(third, 2 * TAIL, axis=1)


def tail_of(joined, field):
    return pltpu.roll(joined, 128 - TAIL * field, axis=1) if field else joined


def pack_kernel(x_ref, spec_ref, leg_ref, o_ref, spec_out, leg_out, held, arrived, rows, fetched):
    fetches = (
        pltpu.make_async_copy(spec_ref, spec_out, fetched.at[0]),
        pltpu.make_async_copy(leg_ref.at[pl.ds(0, PAIR_BLOCK)], leg_out, fetched.at[1]),
    )

    def part(k):
        return pltpu.make_async_copy(x_ref.at[pl.ds(6 * k, 6)], held.at[pl.ds(6 * k, 6)], arrived.at[k])

    for k in range(4):
        part(k).start()
    for fetch in fetches:
        fetch.start()
    for k in range(4):
        part(k).wait()
        for pair in (2 * k, 2 * k + 1):
            tails = []
            for f in range(FIELDS):
                x = held[3 * pair + f].astype(F32)
                rows[pl.ds(3 * pair + f, OWNERS, stride=32), :] = x[:, 0:128]
                tails.append(jnp.concatenate([x[:, 128:COLS], jnp.zeros((OWNERS, 128 - TAIL), F32)], axis=1))
            rows[pl.ds(24 + pair, OWNERS, stride=32), :] = join_tails(*tails)
    for j in range(OWNERS):
        o_ref[j] = rows[32 * j : 32 * j + 32, :].astype(BF16)
    for fetch in fetches:
        fetch.wait()


def pack_rows(x, spec, legendre):
    slots = legendre.shape[2]
    return pl.pallas_call(
        pack_kernel,
        in_specs=[pl.BlockSpec(memory_space=pltpu.HBM)] * 3,
        out_specs=[pl.BlockSpec(memory_space=pltpu.VMEM)] * 3,
        out_shape=[
            jax.ShapeDtypeStruct((OWNERS, 32, 128), BF16),
            pltpu.VMEM((PAIRS, FIELDS, 2, slots), BF16),
            pltpu.VMEM((PAIR_BLOCK, 32, slots), BF16),
        ],
        scratch_shapes=[
            pltpu.VMEM((24, OWNERS, COLS), BF16),
            pltpu.SemaphoreType.DMA((4,)),
            pltpu.VMEM((1024, 128), F32),
            pltpu.SemaphoreType.DMA((2,)),
        ],
        compiler_params=vmem_params(4),
        cost_estimate=pl.CostEstimate(flops=0, bytes_accessed=800_000, transcendentals=0),
        name="pack_rows",
    )(pltpu.with_memory_space_constraint(x, pltpu.HBM), spec, legendre)


def unpack_kernel(x_ref, o_ref, rows):
    for j in range(OWNERS):
        rows[32 * j : 32 * j + 32, :] = x_ref[j].astype(F32)
    for pair in range(8):
        joined = rows[pl.ds(24 + pair, OWNERS, stride=32), :]
        for f in range(FIELDS):
            o_ref[3 * pair + f, :, 0:128] = rows[pl.ds(3 * pair + f, OWNERS, stride=32), :].astype(BF16)
            o_ref[3 * pair + f, :, 128:COLS] = tail_of(joined, f)[:, 0:TAIL].astype(BF16)


def unpack_rows(x):
    return pl.pallas_call(
        unpack_kernel,
        out_shape=jax.ShapeDtypeStruct((24, OWNERS, COLS), BF16),
        scratch_shapes=[pltpu.VMEM((1024, 128), F32)],
        compiler_params=vmem_params(4),
        cost_estimate=pl.CostEstimate(flops=0, bytes_accessed=800_000, transcendentals=0),
        name="unpack_rows",
    )(x)


def legendre_block(leg_ref, held, arrived, k):
    rows = pl.ds(pl.multiple_of(k * PAIR_BLOCK, PAIR_BLOCK), PAIR_BLOCK)
    return pltpu.make_async_copy(leg_ref.at[rows], held.at[rows], arrived.at[k])


def legendre_start(leg_ref, held, arrived):
    for k in range(1, PAIRS // PAIR_BLOCK):
        legendre_block(leg_ref, held, arrived, k).start()


def legendre_inverse_kernel(
    pw_ref, me_ref, leg_ref, block_ref, spec_ref, out_ref, held, arrived, by_pair, by_lat
):
    step = pl.program_id(0)
    slots = leg_ref.shape[2]
    slot = lax.broadcasted_iota(jnp.int32, (8, slots), 1)
    alternate = jnp.where(slot % 2 == 0, 1.0, -1.0).astype(F32)
    valid = slot <= TRUNCATION + 1
    row = lax.broadcasted_iota(jnp.int32, (32, 32), 0)

    def sum_block(table):
        for k in range(PAIR_BLOCK):
            pair = step * PAIR_BLOCK + k
            wave = pw_ref[me_ref[0] * PAIRS + pair]
            first = slot <= TRUNCATION - wave
            a = jnp.concatenate(
                [spec_ref[pair, f].astype(F32) for f in range(FIELDS)] + [jnp.zeros((2, slots), F32)], axis=0
            )
            a = jnp.where(valid, a, 0.0)
            b = a * alternate
            lhs = jnp.concatenate(
                [
                    jnp.where(first, a, 0.0),
                    jnp.where(first, b, 0.0),
                    jnp.where(first, 0.0, a),
                    jnp.where(first, 0.0, b),
                ],
                axis=0,
            ).astype(BF16)
            sums = lax.dot_general(lhs, table(k), NT, preferred_element_type=F32)
            sign = (1 - 2 * (wave % 2)).astype(F32)
            sums = jnp.where(row >= 24, sums * sign, sums)
            by_pair[pl.ds(pair, 32, stride=PAIRS), :] = jnp.concatenate(
                [sums, jnp.zeros((32, 96), F32)], axis=1
            )

    @pl.when(step == 0)
    def _():
        legendre_start(leg_ref, held, arrived)
        sum_block(lambda k: block_ref[k])

    @pl.when(step > 0)
    def _():
        legendre_block(leg_ref, held, arrived, step).wait()
        sum_block(lambda k: held[step * PAIR_BLOCK + k])

    @pl.when(step == pl.num_programs(0) - 1)
    def _():
        for half in range(4):
            h, w = half % 2, half // 2
            for c in range(6):
                start = (half * 8 + c) * PAIRS
                turned = jnp.concatenate(
                    [by_pair[start : start + PAIRS, :], jnp.zeros((48, 128), F32)], axis=0
                ).T
                by_lat[w, pl.ds(h * 6 + (c % 2) * 3 + c // 2, 32, stride=12), :] = turned[0:32, :]
        x, core = me_ref[0] // 2, me_ref[0] % 2
        for s in range(4):
            for d in range(2):
                dest = ((x + s) % 4) * 2 + (core + d) % 2
                rows = pl.ds(pl.multiple_of(dest * 48, 8), 48)
                out_ref[s, d, :, 0:128] = by_lat[0, rows, :].astype(BF16)
                out_ref[s, d, :, 128:256] = by_lat[1, rows, :].astype(BF16)


def legendre_inverse(pair_wave, me, legendre, block, spec):
    slots = legendre.shape[2]
    return pl.pallas_call(
        legendre_inverse_kernel,
        grid_spec=pltpu.PrefetchScalarGridSpec(
            num_scalar_prefetch=2,
            grid=(PAIRS // PAIR_BLOCK,),
            in_specs=[
                pl.BlockSpec(memory_space=pltpu.HBM),
                pl.BlockSpec(memory_space=pltpu.VMEM),
                pl.BlockSpec(memory_space=pltpu.VMEM),
            ],
            out_specs=pl.BlockSpec((4, 2, 48, 256), lambda i, *_: (0, 0, 0, 0)),
            scratch_shapes=[
                pltpu.VMEM((PAIRS, 32, slots), BF16),
                pltpu.SemaphoreType.DMA((PAIRS // PAIR_BLOCK,)),
                pltpu.VMEM((32 * PAIRS, 128), F32),
                pltpu.VMEM((2, 384, 128), F32),
            ],
        ),
        out_shape=jax.ShapeDtypeStruct((4, 2, 48, 256), BF16),
        compiler_params=vmem_params(16),
        cost_estimate=pl.CostEstimate(flops=2 * 80 * 32 * 32 * 1288, bytes_accessed=9_000_000, transcendentals=0),
        name="legendre_inverse",
    )(pair_wave, me, legendre, block, spec)


def join_pieces(pieces):
    lane = lax.broadcasted_iota(jnp.int32, pieces[0].shape, 1)
    rolled = [pltpu.roll(p, (80 * i) % 128, axis=1) if (80 * i) % 128 else p for i, p in enumerate(pieces)]
    tiles = []
    for k in range(10):
        tile = None
        for i in range(16):
            low, high = 80 * i - 128 * k, 80 * i + 80 - 128 * k
            if high <= 0 or low >= 128:
                continue
            tile = rolled[i] if tile is None else jnp.where(lane >= low, rolled[i], tile)
        tiles.append(tile)
    return tiles


def cut_piece(ref, i):
    tile, shift = (80 * i) // 128, (80 * i) % 128
    low = ref[:, tile * 128 : tile * 128 + 128]
    if shift == 0:
        return low
    low = pltpu.roll(low, 128 - shift, axis=1)
    if shift + 80 <= 128:
        return low
    high = pltpu.roll(ref[:, tile * 128 + 128 : tile * 128 + 256], 128 - shift, axis=1)
    lane = lax.broadcasted_iota(jnp.int32, low.shape, 1)
    return jnp.where(lane < 128 - shift, low, high)


def cos_sin(turn, length):
    times = jnp.floor(turn * (1.0 / length) + 0.5)
    u = (turn - times * length) * (math.pi / length)
    u2 = u * u
    s = u * (
        1.0
        + u2
        * (
            -1.0 / 6
            + u2 * (1.0 / 120 + u2 * (-1.0 / 5040 + u2 * (1.0 / 362880 + u2 * (-1.0 / 39916800))))
        )
    )
    c = 1.0 + u2 * (
        -0.5
        + u2
        * (
            1.0 / 24
            + u2
            * (-1.0 / 720 + u2 * (1.0 / 40320 + u2 * (-1.0 / 3628800 + u2 * (1.0 / 479001600))))
        )
    )
    return 1.0 - 2.0 * s * s, 2.0 * s * c


def table_kernel(me_ref, waves_ref, outer_ref, inner_ref, factor_ref, wave_row):
    lat = pl.program_id(0)
    me = me_ref[0]
    x, core = me // 2, me % 2

    @pl.when(lat == 0)
    def _():
        pieces = []
        for d in range(2):
            for s in range(4):
                source = ((x + 4 - s) % 4) * 2 + (core + d) % 2
                for w in range(2):
                    pieces.append(jnp.broadcast_to(waves_ref[source, w : w + 1, :], (8, 128)))
        for k, tile in enumerate(join_pieces(pieces)):
            wave_row[:, 128 * k : 128 * k + 128] = tile
            factor_ref[:, 128 * k : 128 * k + 128] = jnp.where(tile == 0.0, 1.0, 2.0)

    length = (5012 + 16 * me + 4 * lat).astype(F32)
    length = jnp.full((8, WAVES), length, F32)
    wave = wave_row[...]
    eight = lax.broadcasted_iota(jnp.int32, (8, WAVES), 0).astype(F32)
    low_c, low_s = cos_sin(wave * (eight * COLS), length)
    high_c, high_s = cos_sin(wave * (eight * (8 * COLS)), length)
    for k in range(4):
        hc, hs = high_c[k : k + 1, :], high_s[k : k + 1, :]
        outer_ref[0, 0, 8 * k : 8 * k + 8, :] = low_c * hc - low_s * hs
        outer_ref[0, 1, 8 * k : 8 * k + 8, :] = low_s * hc + low_c * hs
    low_c, low_s = cos_sin(wave * eight, length)
    for block in range(3):
        high_c, high_s = cos_sin(wave * (eight * 8.0 + 64.0 * block), length)
        for k in range(0, 8, 2):
            base = 64 * block + 8 * k
            if base >= BROWS:
                continue
            parts_c, parts_s = [], []
            for kk in (k, k + 1):
                hc, hs = high_c[kk : kk + 1, :], high_s[kk : kk + 1, :]
                parts_c.append(low_c * hc - low_s * hs)
                parts_s.append(low_s * hc + low_c * hs)
            inner_ref[0, base : base + 16, 0:WAVES] = jnp.concatenate(parts_c, axis=0).astype(BF16)
            inner_ref[0, base : base + 16, WAVES:] = jnp.concatenate(parts_s, axis=0).astype(BF16)


def phase_tables(me, waves):
    return pl.pallas_call(
        table_kernel,
        grid_spec=pltpu.PrefetchScalarGridSpec(
            num_scalar_prefetch=1,
            grid=(4,),
            in_specs=[pl.BlockSpec((8, 2, 128), lambda i, *_: (0, 0, 0))],
            out_specs=[
                pl.BlockSpec((1, 2, OWNERS, WAVES), lambda i, *_: (i, 0, 0, 0)),
                pl.BlockSpec((1, BROWS, 2 * WAVES), lambda i, *_: (i, 0, 0)),
                pl.BlockSpec((8, WAVES), lambda i, *_: (0, 0)),
            ],
            scratch_shapes=[pltpu.VMEM((8, WAVES), F32)],
        ),
        out_shape=[
            jax.ShapeDtypeStruct((4, 2, OWNERS, WAVES), F32),
            jax.ShapeDtypeStruct((4, BROWS, 2 * WAVES), BF16),
            jax.ShapeDtypeStruct((8, WAVES), F32),
        ],
        compiler_params=vmem_params(8),
        cost_estimate=pl.CostEstimate(flops=40_000_000, bytes_accessed=5_000_000, transcendentals=0),
        name="phase_tables",
    )(me, waves)


def inside_mask(me, lat):
    length = 5012 + 16 * me + 4 * lat
    owner = lax.broadcasted_iota(jnp.int32, (OWNERS, BROWS), 0)
    col = lax.broadcasted_iota(jnp.int32, (OWNERS, BROWS), 1)
    return (col < COLS) & (owner * COLS + col < length)


def row_kernel(
    me_ref,
    weight_ref,
    kept_ref,
    got_ref,
    forcing_ref,
    outer_ref,
    inner_ref,
    factor_ref,
    leg_ref,
    send_ref,
    own_ref,
    other_ref,
    block_ref,
    fetched,
    coeffs,
    turned,
    grid_rows,
    force_rows,
    values,
    samples,
    sums,
):
    lat = pl.program_id(0)
    me = me_ref[0]

    fetch = pltpu.make_async_copy(leg_ref.at[pl.ds(0, PAIR_BLOCK)], block_ref, fetched)

    @pl.when(lat == 0)
    def _():
        fetch.start()
        pieces = []
        for ref in (kept_ref, got_ref):
            for s in range(4):
                for w in range(2):
                    pieces.append(ref[s, :, 128 * w : 128 * w + 128].astype(F32))
        for k, tile in enumerate(join_pieces(pieces)):
            coeffs[:, 128 * k : 128 * k + 128] = tile * factor_ref[0:1, 128 * k : 128 * k + 128]
        for j in range(OWNERS):
            force_rows[32 * j : 32 * j + 32, :] = forcing_ref[j].astype(F32)

    for r in range(6):
        h, f = r // 3, r % 3
        real = coeffs[pl.ds(lat * 12 + h * 6 + f, 1), :]
        imag = coeffs[pl.ds(lat * 12 + h * 6 + 3 + f, 1), :]
        oc, os = outer_ref[lat, 0], outer_ref[lat, 1]
        turned[32 * r : 32 * r + 32, 0:WAVES] = (real * oc - imag * os).astype(BF16)
        turned[32 * r : 32 * r + 32, WAVES:] = (-(real * os + imag * oc)).astype(BF16)
    rows = lax.dot_general(turned[...], inner_ref[lat], NT, preferred_element_type=F32)
    inside = inside_mask(me, lat)
    for r in range(6):
        value = jnp.where(inside, rows[32 * r : 32 * r + 32, :], 0.0).astype(BF16).astype(F32)
        values[32 * r : 32 * r + 32, :] = value
        grid_rows[pl.ds(lat * 6 + r, OWNERS, stride=32), :] = value[:, 0:128]
    for h in range(2):
        tails = [
            jnp.concatenate(
                [values[32 * r : 32 * r + 32, 128:BROWS], jnp.zeros((OWNERS, 256 - BROWS), F32)], axis=1
            )
            for r in range(3 * h, 3 * h + 3)
        ]
        grid_rows[pl.ds(24 + lat * 2 + h, OWNERS, stride=32), :] = join_tails(*tails)
    for r in range(6):
        h, f = r // 3, r % 3
        other = h * 3 + (f + 1) % 3
        product = values[32 * r : 32 * r + 32, :] * values[32 * other : 32 * other + 32, :]
        tail = tail_of(force_rows[pl.ds(24 + lat * 2 + h, OWNERS, stride=32), :], f)
        force = jnp.concatenate(
            [force_rows[pl.ds(lat * 6 + r, OWNERS, stride=32), :], tail[:, 0 : BROWS - 128]], axis=1
        )
        samples[32 * r : 32 * r + 32, :] = jnp.where(inside, product + force, 0.0).astype(BF16)
    length = jnp.full((1, 256), (5012 + 16 * me + 4 * lat).astype(F32), F32)
    scale = weight_ref[me * 4 + lat] * lax.rsqrt(length)
    data = samples[...]
    for n in range(0, WAVES, 256):
        part_c = lax.dot_general(data, inner_ref[lat, :, n : n + 256], NN, preferred_element_type=F32)
        part_s = lax.dot_general(
            data, inner_ref[lat, :, WAVES + n : WAVES + n + 256], NN, preferred_element_type=F32
        )
        oc, os = outer_ref[lat, 0, :, n : n + 256], outer_ref[lat, 1, :, n : n + 256]
        for r in range(6):
            h, f = r // 3, r % 3
            pc, ps = part_c[32 * r : 32 * r + 32, :], part_s[32 * r : 32 * r + 32, :]
            real = jnp.sum(pc * oc - ps * os, axis=0, keepdims=True)
            imag = jnp.sum(ps * oc + pc * os, axis=0, keepdims=True)
            sums[pl.ds(lat * 12 + h * 6 + f, 1), n : n + 256] = real * scale
            sums[pl.ds(lat * 12 + h * 6 + 3 + f, 1), n : n + 256] = -imag * scale

    @pl.when(lat == 3)
    def _():
        for j in range(OWNERS):
            send_ref[j] = grid_rows[32 * j : 32 * j + 32, :].astype(BF16)
        for d, ref in enumerate((own_ref, other_ref)):
            for s in range(4):
                for w in range(2):
                    piece = cut_piece(sums, (d * 4 + s) * 2 + w)
                    ref[s, :, 128 * w : 128 * w + 128] = piece.astype(BF16)
        fetch.wait()


def transform_rows(me, weight, kept, got, forcing, outer, inner, factor, legendre):
    slots = legendre.shape[2]
    return pl.pallas_call(
        row_kernel,
        grid_spec=pltpu.PrefetchScalarGridSpec(
            num_scalar_prefetch=2,
            grid=(4,),
            in_specs=[
                pl.BlockSpec((4, 48, 256), lambda i, *_: (0, 0, 0)),
                pl.BlockSpec((4, 48, 256), lambda i, *_: (0, 0, 0)),
                pl.BlockSpec(memory_space=pltpu.VMEM),
                pl.BlockSpec(memory_space=pltpu.VMEM),
                pl.BlockSpec(memory_space=pltpu.VMEM),
                pl.BlockSpec(memory_space=pltpu.VMEM),
                pl.BlockSpec(memory_space=pltpu.HBM),
            ],
            out_specs=[
                pl.BlockSpec((OWNERS, 32, 128), lambda i, *_: (0, 0, 0)),
                pl.BlockSpec((4, 48, 256), lambda i, *_: (0, 0, 0)),
                pl.BlockSpec((4, 48, 256), lambda i, *_: (0, 0, 0)),
                pl.BlockSpec(memory_space=pltpu.VMEM),
            ],
            scratch_shapes=[
                pltpu.SemaphoreType.DMA,
                pltpu.VMEM((48, WAVES), F32),
                pltpu.VMEM((192, 2 * WAVES), BF16),
                pltpu.VMEM((1024, 128), F32),
                pltpu.VMEM((1024, 128), F32),
                pltpu.VMEM((192, BROWS), F32),
                pltpu.VMEM((192, BROWS), BF16),
                pltpu.VMEM((48, WAVES), F32),
            ],
        ),
        out_shape=[
            jax.ShapeDtypeStruct((OWNERS, 32, 128), BF16),
            jax.ShapeDtypeStruct((4, 48, 256), BF16),
            jax.ShapeDtypeStruct((4, 48, 256), BF16),
            pltpu.VMEM((PAIR_BLOCK, 32, slots), BF16),
        ],
        compiler_params=vmem_params(14),
        cost_estimate=pl.CostEstimate(flops=1_400_000_000, bytes_accessed=6_000_000, transcendentals=0),
        name="transform_rows",
    )(
        me,
        weight,
        kept,
        got,
        forcing,
        outer,
        inner,
        factor,
        legendre,
    )


def legendre_direct_kernel(
    pw_ref, me_ref, first_ref, second_ref, third_ref, fourth_ref, leg_ref, block_ref, out_ref, held, arrived, by_lat, by_pair
):
    step = pl.program_id(0)
    slots = leg_ref.shape[2]

    @pl.when(step == 0)
    def _():
        legendre_start(leg_ref, held, arrived)
        x, core = me_ref[0] // 2, me_ref[0] % 2
        for s, ref in enumerate((first_ref, second_ref, third_ref, fourth_ref)):
            for d in range(2):
                source = ((x + s) % 4) * 2 + (core + d) % 2
                rows = pl.ds(pl.multiple_of(source * 48, 8), 48)
                for w in range(2):
                    by_lat[w, rows, :] = ref[d, :, 128 * w : 128 * w + 128].astype(F32)
        for w in range(2):
            for c in range(6):
                north = by_lat[w, pl.ds(c, 32, stride=12), :]
                south = by_lat[w, pl.ds(6 + c, 32, stride=12), :]
                for odd, value in enumerate((north + south, north - south)):
                    turned = jnp.concatenate([value, jnp.zeros((96, 128), F32)], axis=0).T
                    row = (w * 2 + odd) * 8 + (c % 3) * 2 + c // 3
                    by_pair[pl.ds(row, PAIRS, stride=32), :] = turned[0:PAIRS, :]

    slot = lax.broadcasted_iota(jnp.int32, (8, slots), 1)
    even = slot % 2 == 0
    valid = slot <= TRUNCATION + 1

    def sum_block(table):
        for k in range(PAIR_BLOCK):
            pair = step * PAIR_BLOCK + k
            wave = pw_ref[me_ref[0] * PAIRS + pair]
            lhs = by_pair[pl.ds(pl.multiple_of(pair * 32, 32), 32), :][:, 0:32].astype(BF16)
            sums = lax.dot_general(lhs, table(k), NN, preferred_element_type=F32)
            first = jnp.where(even, sums[0:8], sums[8:16])
            second = jnp.where((slot + wave) % 2 == 0, sums[16:24], sums[24:32])
            value = jnp.where(slot <= TRUNCATION - wave, first, second)
            value = jnp.where(valid, value, 0.0).astype(BF16)
            for f in range(FIELDS):
                out_ref[k, f] = value[2 * f : 2 * f + 2]

    @pl.when(step == 0)
    def _():
        sum_block(lambda k: block_ref[k])

    @pl.when(step > 0)
    def _():
        legendre_block(leg_ref, held, arrived, step).wait()
        sum_block(lambda k: held[step * PAIR_BLOCK + k])


def legendre_direct(pair_wave, me, came, legendre, block):
    slots = legendre.shape[2]
    return pl.pallas_call(
        legendre_direct_kernel,
        grid_spec=pltpu.PrefetchScalarGridSpec(
            num_scalar_prefetch=2,
            grid=(PAIRS // PAIR_BLOCK,),
            in_specs=[pl.BlockSpec((2, 48, 256), lambda i, *_: (0, 0, 0))] * 4
            + [pl.BlockSpec(memory_space=pltpu.HBM), pl.BlockSpec(memory_space=pltpu.VMEM)],
            out_specs=pl.BlockSpec((PAIR_BLOCK, FIELDS, 2, slots), lambda i, *_: (i, 0, 0, 0)),
            scratch_shapes=[
                pltpu.VMEM((PAIRS, 32, slots), BF16),
                pltpu.SemaphoreType.DMA((PAIRS // PAIR_BLOCK,)),
                pltpu.VMEM((2, 384, 128), F32),
                pltpu.VMEM((32 * PAIRS, 128), F32),
            ],
        ),
        out_shape=jax.ShapeDtypeStruct((PAIRS, FIELDS, 2, slots), BF16),
        compiler_params=vmem_params(16),
        cost_estimate=pl.CostEstimate(flops=2 * 80 * 32 * 32 * 1288, bytes_accessed=9_000_000, transcendentals=0),
        name="legendre_direct",
    )(pair_wave, me, *came, legendre, block)


def to_chip(value, distance):
    return lax.ppermute(value, "aa", [(i, ((i // 2 + distance) % 4) * 2 + i % 2) for i in range(8)])


def to_other_core(value):
    return lax.ppermute(value, "aa", [(i, i ^ 1) for i in range(8)])


def per_device(spec_in, legendre, pair_wave, quad_weight, forcing):
    me = lax.axis_index("aa").astype(jnp.int32).reshape(1)
    legendre = pltpu.with_memory_space_constraint(legendre, pltpu.HBM)
    wave_table = pltpu.with_memory_space_constraint(pair_wave, pltpu.HBM)
    spec = jnp.swapaxes(spec_in.reshape(PAIRS, 2, FIELDS, -1), 1, 2)
    spec = pltpu.with_memory_space_constraint(spec, pltpu.HBM)
    forcing_send, spec, block = pack_rows(forcing.reshape(24, OWNERS, COLS), spec, legendre)
    forcing_here = lax.all_to_all(forcing_send, "ba", split_axis=0, concat_axis=0, tiled=True)
    fourier = legendre_inverse(wave_table, me, legendre, block, spec)
    pairs = pair_wave.astype(F32).reshape(8, PAIRS)
    waves = jnp.pad(jnp.stack([pairs, TRUNCATION - pairs], axis=1), ((0, 0), (0, 0), (0, 48)))
    waves, forcing_here = lax.optimization_barrier((waves, forcing_here))
    outer, inner, factor = phase_tables(me, waves)
    came = [fourier[0]] + [to_chip(fourier[s], s) for s in range(1, 4)]
    *came, factor = lax.optimization_barrier((*came, factor))
    kept = jnp.stack([c[0] for c in came])
    got = to_other_core(jnp.stack([c[1] for c in came]))
    grid_send, own, other, block = transform_rows(
        me, quad_weight, kept, got, forcing_here, outer, inner, factor, legendre
    )
    grid_came = lax.all_to_all(grid_send, "ba", split_axis=0, concat_axis=0, tiled=True)
    passed = to_other_core(other)
    parts = [jnp.stack([own[s], passed[s]]) for s in range(4)]
    came = [parts[0]] + [to_chip(parts[s], -s) for s in range(1, 4)]
    spec_out = legendre_direct(wave_table, me, came, legendre, block)
    grid = unpack_rows(grid_came)
    return (
        grid.reshape(8, FIELDS, OWNERS, COLS),
        jnp.swapaxes(spec_out, 1, 2).reshape(PAIRS, 2, FIELDS, 1, -1),
    )


def solution(mesh):
    placed = (
        P("aa", None, None, "ba", None),
        P("aa", None, None),
        P(),
        P(),
        P("aa", None, None, "ba"),
    )
    return jax.shard_map(
        per_device,
        mesh=mesh,
        in_specs=placed,
        out_specs=(P("aa", None, None, "ba"), P("aa", None, None, "ba", None)),
        check_vma=False,
    )
```

```python
import functools
import math

import jax
import jax.numpy as jnp
from jax import lax
from jax.experimental import pallas as pl
from jax.experimental.pallas import tpu as pltpu
from jax.sharding import PartitionSpec as P

TRUNCATION = 1279
FIELDS = 3
PAIRS = 80
WAVES = 1280
COLS = 164
OWNERS = 32
BROWS = 176
TAIL = COLS - 128
PAIR_BLOCK = 16
F32 = jnp.float32
BF16 = jnp.bfloat16
NT = (((1,), (1,)), ((), ()))
NN = (((1,), (0,)), ((), ()))


def vmem_params(mib):
    return pltpu.CompilerParams(vmem_limit_bytes=mib << 20)


def join_tails(first, second, third):
    return first + pltpu.roll(second, TAIL, axis=1) + pltpu.roll(third, 2 * TAIL, axis=1)


def tail_of(joined, field):
    return pltpu.roll(joined, 128 - TAIL * field, axis=1) if field else joined


def pack_kernel(x_ref, spec_ref, leg_ref, o_ref, spec_out, leg_out, held, arrived, rows, fetched):
    fetches = (
        pltpu.make_async_copy(spec_ref, spec_out, fetched.at[0]),
        pltpu.make_async_copy(leg_ref.at[pl.ds(0, PAIR_BLOCK)], leg_out, fetched.at[1]),
    )

    def part(k):
        return pltpu.make_async_copy(x_ref.at[pl.ds(6 * k, 6)], held.at[pl.ds(6 * k, 6)], arrived.at[k])

    for k in range(4):
        part(k).start()
    for fetch in fetches:
        fetch.start()
    for k in range(4):
        part(k).wait()
        for pair in (2 * k, 2 * k + 1):
            tails = []
            for f in range(FIELDS):
                x = held[3 * pair + f].astype(F32)
                rows[pl.ds(3 * pair + f, OWNERS, stride=32), :] = x[:, 0:128]
                tails.append(jnp.concatenate([x[:, 128:COLS], jnp.zeros((OWNERS, 128 - TAIL), F32)], axis=1))
            rows[pl.ds(24 + pair, OWNERS, stride=32), :] = join_tails(*tails)
    for j in range(OWNERS):
        o_ref[j] = rows[32 * j : 32 * j + 32, :].astype(BF16)
    for fetch in fetches:
        fetch.wait()


def pack_rows(x, spec, legendre):
    slots = legendre.shape[2]
    return pl.pallas_call(
        pack_kernel,
        in_specs=[pl.BlockSpec(memory_space=pltpu.HBM)] * 3,
        out_specs=[pl.BlockSpec(memory_space=pltpu.VMEM)] * 3,
        out_shape=[
            jax.ShapeDtypeStruct((OWNERS, 32, 128), BF16),
            pltpu.VMEM((PAIRS, FIELDS, 2, slots), BF16),
            pltpu.VMEM((PAIR_BLOCK, 32, slots), BF16),
        ],
        scratch_shapes=[
            pltpu.VMEM((24, OWNERS, COLS), BF16),
            pltpu.SemaphoreType.DMA((4,)),
            pltpu.VMEM((1024, 128), F32),
            pltpu.SemaphoreType.DMA((2,)),
        ],
        compiler_params=vmem_params(4),
        cost_estimate=pl.CostEstimate(flops=0, bytes_accessed=800_000, transcendentals=0),
        name="pack_rows",
    )(pltpu.with_memory_space_constraint(x, pltpu.HBM), spec, legendre)


def unpack_kernel(x_ref, o_ref, rows):
    for j in range(OWNERS):
        rows[32 * j : 32 * j + 32, :] = x_ref[j].astype(F32)
    for pair in range(8):
        joined = rows[pl.ds(24 + pair, OWNERS, stride=32), :]
        for f in range(FIELDS):
            o_ref[3 * pair + f, :, 0:128] = rows[pl.ds(3 * pair + f, OWNERS, stride=32), :].astype(BF16)
            o_ref[3 * pair + f, :, 128:COLS] = tail_of(joined, f)[:, 0:TAIL].astype(BF16)


def unpack_rows(x):
    return pl.pallas_call(
        unpack_kernel,
        out_shape=jax.ShapeDtypeStruct((24, OWNERS, COLS), BF16),
        scratch_shapes=[pltpu.VMEM((1024, 128), F32)],
        compiler_params=vmem_params(4),
        cost_estimate=pl.CostEstimate(flops=0, bytes_accessed=800_000, transcendentals=0),
        name="unpack_rows",
    )(x)


def legendre_block(leg_ref, held, arrived, k):
    rows = pl.ds(pl.multiple_of(k * PAIR_BLOCK, PAIR_BLOCK), PAIR_BLOCK)
    return pltpu.make_async_copy(leg_ref.at[rows], held.at[rows], arrived.at[k])


def legendre_start(leg_ref, held, arrived):
    for k in range(1, PAIRS // PAIR_BLOCK):
        legendre_block(leg_ref, held, arrived, k).start()


def legendre_inverse_kernel(
    pw_ref, me_ref, leg_ref, block_ref, spec_ref, out_ref, held, arrived, by_pair, by_lat
):
    step = pl.program_id(0)
    slots = leg_ref.shape[2]
    slot = lax.broadcasted_iota(jnp.int32, (8, slots), 1)
    alternate = jnp.where(slot % 2 == 0, 1.0, -1.0).astype(F32)
    valid = slot <= TRUNCATION + 1
    row = lax.broadcasted_iota(jnp.int32, (32, 32), 0)

    def sum_block(table):
        for k in range(PAIR_BLOCK):
            pair = step * PAIR_BLOCK + k
            wave = pw_ref[me_ref[0] * PAIRS + pair]
            first = slot <= TRUNCATION - wave
            a = jnp.concatenate(
                [spec_ref[pair, f].astype(F32) for f in range(FIELDS)] + [jnp.zeros((2, slots), F32)], axis=0
            )
            a = jnp.where(valid, a, 0.0)
            b = a * alternate
            lhs = jnp.concatenate(
                [
                    jnp.where(first, a, 0.0),
                    jnp.where(first, b, 0.0),
                    jnp.where(first, 0.0, a),
                    jnp.where(first, 0.0, b),
                ],
                axis=0,
            ).astype(BF16)
            sums = lax.dot_general(lhs, table(k), NT, preferred_element_type=F32)
            sign = (1 - 2 * (wave % 2)).astype(F32)
            sums = jnp.where(row >= 24, sums * sign, sums)
            by_pair[pl.ds(pair, 32, stride=PAIRS), :] = jnp.concatenate(
                [sums, jnp.zeros((32, 96), F32)], axis=1
            )

    @pl.when(step == 0)
    def _():
        legendre_start(leg_ref, held, arrived)
        sum_block(lambda k: block_ref[k])

    @pl.when(step > 0)
    def _():
        legendre_block(leg_ref, held, arrived, step).wait()
        sum_block(lambda k: held[step * PAIR_BLOCK + k])

    @pl.when(step == pl.num_programs(0) - 1)
    def _():
        for half in range(4):
            h, w = half % 2, half // 2
            for c in range(6):
                start = (half * 8 + c) * PAIRS
                turned = jnp.concatenate(
                    [by_pair[start : start + PAIRS, :], jnp.zeros((48, 128), F32)], axis=0
                ).T
                by_lat[w, pl.ds(h * 6 + (c % 2) * 3 + c // 2, 32, stride=12), :] = turned[0:32, :]
        x, core = me_ref[0] // 2, me_ref[0] % 2
        for s in range(4):
            for d in range(2):
                dest = ((x + s) % 4) * 2 + (core + d) % 2
                rows = pl.ds(pl.multiple_of(dest * 48, 8), 48)
                out_ref[s, d, :, 0:128] = by_lat[0, rows, :].astype(BF16)
                out_ref[s, d, :, 128:256] = by_lat[1, rows, :].astype(BF16)


def legendre_inverse(pair_wave, me, legendre, block, spec):
    slots = legendre.shape[2]
    return pl.pallas_call(
        legendre_inverse_kernel,
        grid_spec=pltpu.PrefetchScalarGridSpec(
            num_scalar_prefetch=2,
            grid=(PAIRS // PAIR_BLOCK,),
            in_specs=[
                pl.BlockSpec(memory_space=pltpu.HBM),
                pl.BlockSpec(memory_space=pltpu.VMEM),
                pl.BlockSpec(memory_space=pltpu.VMEM),
            ],
            out_specs=pl.BlockSpec((4, 2, 48, 256), lambda i, *_: (0, 0, 0, 0)),
            scratch_shapes=[
                pltpu.VMEM((PAIRS, 32, slots), BF16),
                pltpu.SemaphoreType.DMA((PAIRS // PAIR_BLOCK,)),
                pltpu.VMEM((32 * PAIRS, 128), F32),
                pltpu.VMEM((2, 384, 128), F32),
            ],
        ),
        out_shape=jax.ShapeDtypeStruct((4, 2, 48, 256), BF16),
        compiler_params=vmem_params(16),
        cost_estimate=pl.CostEstimate(flops=2 * 80 * 32 * 32 * 1288, bytes_accessed=9_000_000, transcendentals=0),
        name="legendre_inverse",
    )(pair_wave, me, legendre, block, spec)


def join_pieces(pieces):
    lane = lax.broadcasted_iota(jnp.int32, pieces[0].shape, 1)
    rolled = [pltpu.roll(p, (80 * i) % 128, axis=1) if (80 * i) % 128 else p for i, p in enumerate(pieces)]
    tiles = []
    for k in range(10):
        tile = None
        for i in range(16):
            low, high = 80 * i - 128 * k, 80 * i + 80 - 128 * k
            if high <= 0 or low >= 128:
                continue
            tile = rolled[i] if tile is None else jnp.where(lane >= low, rolled[i], tile)
        tiles.append(tile)
    return tiles


def cut_piece(ref, i):
    tile, shift = (80 * i) // 128, (80 * i) % 128
    low = ref[:, tile * 128 : tile * 128 + 128]
    if shift == 0:
        return low
    low = pltpu.roll(low, 128 - shift, axis=1)
    if shift + 80 <= 128:
        return low
    high = pltpu.roll(ref[:, tile * 128 + 128 : tile * 128 + 256], 128 - shift, axis=1)
    lane = lax.broadcasted_iota(jnp.int32, low.shape, 1)
    return jnp.where(lane < 128 - shift, low, high)


def cos_sin(turn, length):
    times = jnp.floor(turn * (1.0 / length) + 0.5)
    u = (turn - times * length) * (math.pi / length)
    u2 = u * u
    s = u * (
        1.0
        + u2
        * (
            -1.0 / 6
            + u2 * (1.0 / 120 + u2 * (-1.0 / 5040 + u2 * (1.0 / 362880 + u2 * (-1.0 / 39916800))))
        )
    )
    c = 1.0 + u2 * (
        -0.5
        + u2
        * (
            1.0 / 24
            + u2
            * (-1.0 / 720 + u2 * (1.0 / 40320 + u2 * (-1.0 / 3628800 + u2 * (1.0 / 479001600))))
        )
    )
    return 1.0 - 2.0 * s * s, 2.0 * s * c


def table_kernel(me_ref, waves_ref, outer_ref, inner_ref, factor_ref, wave_row):
    lat = pl.program_id(0)
    me = me_ref[0]
    x, core = me // 2, me % 2

    @pl.when(lat == 0)
    def _():
        pieces = []
        for d in range(2):
            for s in range(4):
                source = ((x + 4 - s) % 4) * 2 + (core + d) % 2
                for w in range(2):
                    pieces.append(jnp.broadcast_to(waves_ref[source, w : w + 1, :], (8, 128)))
        for k, tile in enumerate(join_pieces(pieces)):
            wave_row[:, 128 * k : 128 * k + 128] = tile
            factor_ref[:, 128 * k : 128 * k + 128] = jnp.where(tile == 0.0, 1.0, 2.0)

    length = (5012 + 16 * me + 4 * lat).astype(F32)
    length = jnp.full((8, WAVES), length, F32)
    wave = wave_row[...]
    eight = lax.broadcasted_iota(jnp.int32, (8, WAVES), 0).astype(F32)
    low_c, low_s = cos_sin(wave * (eight * COLS), length)
    high_c, high_s = cos_sin(wave * (eight * (8 * COLS)), length)
    for k in range(4):
        hc, hs = high_c[k : k + 1, :], high_s[k : k + 1, :]
        outer_ref[0, 0, 8 * k : 8 * k + 8, :] = low_c * hc - low_s * hs
        outer_ref[0, 1, 8 * k : 8 * k + 8, :] = low_s * hc + low_c * hs
    low_c, low_s = cos_sin(wave * eight, length)
    for block in range(3):
        high_c, high_s = cos_sin(wave * (eight * 8.0 + 64.0 * block), length)
        for k in range(0, 8, 2):
            base = 64 * block + 8 * k
            if base >= BROWS:
                continue
            parts_c, parts_s = [], []
            for kk in (k, k + 1):
                hc, hs = high_c[kk : kk + 1, :], high_s[kk : kk + 1, :]
                parts_c.append(low_c * hc - low_s * hs)
                parts_s.append(low_s * hc + low_c * hs)
            inner_ref[0, base : base + 16, 0:WAVES] = jnp.concatenate(parts_c, axis=0).astype(BF16)
            inner_ref[0, base : base + 16, WAVES:] = jnp.concatenate(parts_s, axis=0).astype(BF16)


def phase_tables(me, waves):
    return pl.pallas_call(
        table_kernel,
        grid_spec=pltpu.PrefetchScalarGridSpec(
            num_scalar_prefetch=1,
            grid=(4,),
            in_specs=[pl.BlockSpec((8, 2, 128), lambda i, *_: (0, 0, 0))],
            out_specs=[
                pl.BlockSpec((1, 2, OWNERS, WAVES), lambda i, *_: (i, 0, 0, 0)),
                pl.BlockSpec((1, BROWS, 2 * WAVES), lambda i, *_: (i, 0, 0)),
                pl.BlockSpec((8, WAVES), lambda i, *_: (0, 0)),
            ],
            scratch_shapes=[pltpu.VMEM((8, WAVES), F32)],
        ),
        out_shape=[
            jax.ShapeDtypeStruct((4, 2, OWNERS, WAVES), F32),
            jax.ShapeDtypeStruct((4, BROWS, 2 * WAVES), BF16),
            jax.ShapeDtypeStruct((8, WAVES), F32),
        ],
        compiler_params=vmem_params(8),
        cost_estimate=pl.CostEstimate(flops=40_000_000, bytes_accessed=5_000_000, transcendentals=0),
        name="phase_tables",
    )(me, waves)


def inside_mask(me, lat):
    length = 5012 + 16 * me + 4 * lat
    owner = lax.broadcasted_iota(jnp.int32, (OWNERS, BROWS), 0)
    col = lax.broadcasted_iota(jnp.int32, (OWNERS, BROWS), 1)
    return (col < COLS) & (owner * COLS + col < length)


def row_kernel(
    me_ref,
    weight_ref,
    kept_ref,
    got_ref,
    forcing_ref,
    outer_ref,
    inner_ref,
    factor_ref,
    leg_ref,
    send_ref,
    own_ref,
    other_ref,
    block_ref,
    fetched,
    coeffs,
    turned,
    grid_rows,
    force_rows,
    values,
    samples,
    sums,
):
    lat = pl.program_id(0)
    me = me_ref[0]

    fetch = pltpu.make_async_copy(leg_ref.at[pl.ds(0, PAIR_BLOCK)], block_ref, fetched)

    @pl.when(lat == 0)
    def _():
        fetch.start()
        pieces = []
        for ref in (kept_ref, got_ref):
            for s in range(4):
                for w in range(2):
                    pieces.append(ref[s, :, 128 * w : 128 * w + 128].astype(F32))
        for k, tile in enumerate(join_pieces(pieces)):
            coeffs[:, 128 * k : 128 * k + 128] = tile * factor_ref[0:1, 128 * k : 128 * k + 128]
        for j in range(OWNERS):
            force_rows[32 * j : 32 * j + 32, :] = forcing_ref[j].astype(F32)

    for r in range(6):
        h, f = r // 3, r % 3
        real = coeffs[pl.ds(lat * 12 + h * 6 + f, 1), :]
        imag = coeffs[pl.ds(lat * 12 + h * 6 + 3 + f, 1), :]
        oc, os = outer_ref[lat, 0], outer_ref[lat, 1]
        turned[32 * r : 32 * r + 32, 0:WAVES] = (real * oc - imag * os).astype(BF16)
        turned[32 * r : 32 * r + 32, WAVES:] = (-(real * os + imag * oc)).astype(BF16)
    rows = lax.dot_general(turned[...], inner_ref[lat], NT, preferred_element_type=F32)
    inside = inside_mask(me, lat)
    for r in range(6):
        value = jnp.where(inside, rows[32 * r : 32 * r + 32, :], 0.0).astype(BF16).astype(F32)
        values[32 * r : 32 * r + 32, :] = value
        grid_rows[pl.ds(lat * 6 + r, OWNERS, stride=32), :] = value[:, 0:128]
    for h in range(2):
        tails = [
            jnp.concatenate(
                [values[32 * r : 32 * r + 32, 128:BROWS], jnp.zeros((OWNERS, 256 - BROWS), F32)], axis=1
            )
            for r in range(3 * h, 3 * h + 3)
        ]
        grid_rows[pl.ds(24 + lat * 2 + h, OWNERS, stride=32), :] = join_tails(*tails)
    for r in range(6):
        h, f = r // 3, r % 3
        other = h * 3 + (f + 1) % 3
        product = values[32 * r : 32 * r + 32, :] * values[32 * other : 32 * other + 32, :]
        tail = tail_of(force_rows[pl.ds(24 + lat * 2 + h, OWNERS, stride=32), :], f)
        force = jnp.concatenate(
            [force_rows[pl.ds(lat * 6 + r, OWNERS, stride=32), :], tail[:, 0 : BROWS - 128]], axis=1
        )
        samples[32 * r : 32 * r + 32, :] = jnp.where(inside, product + force, 0.0).astype(BF16)
    length = jnp.full((1, 256), (5012 + 16 * me + 4 * lat).astype(F32), F32)
    scale = weight_ref[me * 4 + lat] * lax.rsqrt(length)
    data = samples[...]
    for n in range(0, WAVES, 256):
        part_c = lax.dot_general(data, inner_ref[lat, :, n : n + 256], NN, preferred_element_type=F32)
        part_s = lax.dot_general(
            data, inner_ref[lat, :, WAVES + n : WAVES + n + 256], NN, preferred_element_type=F32
        )
        oc, os = outer_ref[lat, 0, :, n : n + 256], outer_ref[lat, 1, :, n : n + 256]
        for r in range(6):
            h, f = r // 3, r % 3
            pc, ps = part_c[32 * r : 32 * r + 32, :], part_s[32 * r : 32 * r + 32, :]
            real = jnp.sum(pc * oc - ps * os, axis=0, keepdims=True)
            imag = jnp.sum(ps * oc + pc * os, axis=0, keepdims=True)
            sums[pl.ds(lat * 12 + h * 6 + f, 1), n : n + 256] = real * scale
            sums[pl.ds(lat * 12 + h * 6 + 3 + f, 1), n : n + 256] = -imag * scale

    @pl.when(lat == 3)
    def _():
        for j in range(OWNERS):
            send_ref[j] = grid_rows[32 * j : 32 * j + 32, :].astype(BF16)
        for d, ref in enumerate((own_ref, other_ref)):
            for s in range(4):
                for w in range(2):
                    piece = cut_piece(sums, (d * 4 + s) * 2 + w)
                    ref[s, :, 128 * w : 128 * w + 128] = piece.astype(BF16)
        fetch.wait()


def transform_rows(me, weight, kept, got, forcing, outer, inner, factor, legendre):
    slots = legendre.shape[2]
    return pl.pallas_call(
        row_kernel,
        grid_spec=pltpu.PrefetchScalarGridSpec(
            num_scalar_prefetch=2,
            grid=(4,),
            in_specs=[
                pl.BlockSpec((4, 48, 256), lambda i, *_: (0, 0, 0)),
                pl.BlockSpec((4, 48, 256), lambda i, *_: (0, 0, 0)),
                pl.BlockSpec(memory_space=pltpu.VMEM),
                pl.BlockSpec(memory_space=pltpu.VMEM),
                pl.BlockSpec(memory_space=pltpu.VMEM),
                pl.BlockSpec(memory_space=pltpu.VMEM),
                pl.BlockSpec(memory_space=pltpu.HBM),
            ],
            out_specs=[
                pl.BlockSpec((OWNERS, 32, 128), lambda i, *_: (0, 0, 0)),
                pl.BlockSpec((4, 48, 256), lambda i, *_: (0, 0, 0)),
                pl.BlockSpec((4, 48, 256), lambda i, *_: (0, 0, 0)),
                pl.BlockSpec(memory_space=pltpu.VMEM),
            ],
            scratch_shapes=[
                pltpu.SemaphoreType.DMA,
                pltpu.VMEM((48, WAVES), F32),
                pltpu.VMEM((192, 2 * WAVES), BF16),
                pltpu.VMEM((1024, 128), F32),
                pltpu.VMEM((1024, 128), F32),
                pltpu.VMEM((192, BROWS), F32),
                pltpu.VMEM((192, BROWS), BF16),
                pltpu.VMEM((48, WAVES), F32),
            ],
        ),
        out_shape=[
            pltpu.HBM((OWNERS, 32, 128), BF16),
            jax.ShapeDtypeStruct((4, 48, 256), BF16),
            jax.ShapeDtypeStruct((4, 48, 256), BF16),
            pltpu.VMEM((PAIR_BLOCK, 32, slots), BF16),
        ],
        compiler_params=vmem_params(14),
        cost_estimate=pl.CostEstimate(flops=1_400_000_000, bytes_accessed=6_000_000, transcendentals=0),
        name="transform_rows",
    )(
        me,
        weight,
        kept,
        got,
        forcing,
        outer,
        inner,
        factor,
        legendre,
    )


def legendre_direct_kernel(
    pw_ref, me_ref, first_ref, second_ref, third_ref, fourth_ref, leg_ref, block_ref, out_ref, held, arrived, by_lat, by_pair
):
    step = pl.program_id(0)
    slots = leg_ref.shape[2]

    @pl.when(step == 0)
    def _():
        legendre_start(leg_ref, held, arrived)
        x, core = me_ref[0] // 2, me_ref[0] % 2
        for s, ref in enumerate((first_ref, second_ref, third_ref, fourth_ref)):
            for d in range(2):
                source = ((x + s) % 4) * 2 + (core + d) % 2
                rows = pl.ds(pl.multiple_of(source * 48, 8), 48)
                for w in range(2):
                    by_lat[w, rows, :] = ref[d, :, 128 * w : 128 * w + 128].astype(F32)
        for w in range(2):
            for c in range(6):
                north = by_lat[w, pl.ds(c, 32, stride=12), :]
                south = by_lat[w, pl.ds(6 + c, 32, stride=12), :]
                for odd, value in enumerate((north + south, north - south)):
                    turned = jnp.concatenate([value, jnp.zeros((96, 128), F32)], axis=0).T
                    row = (w * 2 + odd) * 8 + (c % 3) * 2 + c // 3
                    by_pair[pl.ds(row, PAIRS, stride=32), :] = turned[0:PAIRS, :]

    slot = lax.broadcasted_iota(jnp.int32, (8, slots), 1)
    even = slot % 2 == 0
    valid = slot <= TRUNCATION + 1

    def sum_block(table):
        for k in range(PAIR_BLOCK):
            pair = step * PAIR_BLOCK + k
            wave = pw_ref[me_ref[0] * PAIRS + pair]
            lhs = by_pair[pl.ds(pl.multiple_of(pair * 32, 32), 32), :][:, 0:32].astype(BF16)
            sums = lax.dot_general(lhs, table(k), NN, preferred_element_type=F32)
            first = jnp.where(even, sums[0:8], sums[8:16])
            second = jnp.where((slot + wave) % 2 == 0, sums[16:24], sums[24:32])
            value = jnp.where(slot <= TRUNCATION - wave, first, second)
            value = jnp.where(valid, value, 0.0).astype(BF16)
            for f in range(FIELDS):
                out_ref[k, f] = value[2 * f : 2 * f + 2]

    @pl.when(step == 0)
    def _():
        sum_block(lambda k: block_ref[k])

    @pl.when(step > 0)
    def _():
        legendre_block(leg_ref, held, arrived, step).wait()
        sum_block(lambda k: held[step * PAIR_BLOCK + k])


def legendre_direct(pair_wave, me, came, legendre, block):
    slots = legendre.shape[2]
    return pl.pallas_call(
        legendre_direct_kernel,
        grid_spec=pltpu.PrefetchScalarGridSpec(
            num_scalar_prefetch=2,
            grid=(PAIRS // PAIR_BLOCK,),
            in_specs=[pl.BlockSpec((2, 48, 256), lambda i, *_: (0, 0, 0))] * 4
            + [pl.BlockSpec(memory_space=pltpu.HBM), pl.BlockSpec(memory_space=pltpu.VMEM)],
            out_specs=pl.BlockSpec((PAIR_BLOCK, FIELDS, 2, slots), lambda i, *_: (i, 0, 0, 0)),
            scratch_shapes=[
                pltpu.VMEM((PAIRS, 32, slots), BF16),
                pltpu.SemaphoreType.DMA((PAIRS // PAIR_BLOCK,)),
                pltpu.VMEM((2, 384, 128), F32),
                pltpu.VMEM((32 * PAIRS, 128), F32),
            ],
        ),
        out_shape=jax.ShapeDtypeStruct((PAIRS, FIELDS, 2, slots), BF16),
        compiler_params=vmem_params(16),
        cost_estimate=pl.CostEstimate(flops=2 * 80 * 32 * 32 * 1288, bytes_accessed=9_000_000, transcendentals=0),
        name="legendre_direct",
    )(pair_wave, me, *came, legendre, block)


def to_chip(value, distance):
    return lax.ppermute(value, "aa", [(i, ((i // 2 + distance) % 4) * 2 + i % 2) for i in range(8)])


def to_other_core(value):
    return lax.ppermute(value, "aa", [(i, i ^ 1) for i in range(8)])


def per_device(spec_in, legendre, pair_wave, quad_weight, forcing):
    me = lax.axis_index("aa").astype(jnp.int32).reshape(1)
    legendre = pltpu.with_memory_space_constraint(legendre, pltpu.HBM)
    wave_table = pltpu.with_memory_space_constraint(pair_wave, pltpu.HBM)
    spec = jnp.swapaxes(spec_in.reshape(PAIRS, 2, FIELDS, -1), 1, 2)
    spec = pltpu.with_memory_space_constraint(spec, pltpu.HBM)
    forcing_send, spec, block = pack_rows(forcing.reshape(24, OWNERS, COLS), spec, legendre)
    forcing_here = lax.all_to_all(forcing_send, "ba", split_axis=0, concat_axis=0, tiled=True)
    fourier = legendre_inverse(wave_table, me, legendre, block, spec)
    pairs = pair_wave.astype(F32).reshape(8, PAIRS)
    waves = jnp.pad(jnp.stack([pairs, TRUNCATION - pairs], axis=1), ((0, 0), (0, 0), (0, 48)))
    waves, forcing_here = lax.optimization_barrier((waves, forcing_here))
    outer, inner, factor = phase_tables(me, waves)
    came = [fourier[0]] + [to_chip(fourier[s], s) for s in range(1, 4)]
    *came, factor = lax.optimization_barrier((*came, factor))
    kept = jnp.stack([c[0] for c in came])
    got = to_other_core(jnp.stack([c[1] for c in came]))
    grid_send, own, other, block = transform_rows(
        me, quad_weight, kept, got, forcing_here, outer, inner, factor, legendre
    )
    staying, grid_send = lax.optimization_barrier((own[0], grid_send))
    grid_came = lax.all_to_all(grid_send, "ba", split_axis=0, concat_axis=0, tiled=True)
    passed = to_other_core(other)
    parts = [jnp.stack([own[s] if s else staying, passed[s]]) for s in range(4)]
    came = [parts[0]] + [to_chip(parts[s], -s) for s in range(1, 4)]
    spec_out = legendre_direct(wave_table, me, came, legendre, block)
    grid = unpack_rows(grid_came)
    return (
        grid.reshape(8, FIELDS, OWNERS, COLS),
        jnp.swapaxes(spec_out, 1, 2).reshape(PAIRS, 2, FIELDS, 1, -1),
    )


def solution(mesh):
    placed = (
        P("aa", None, None, "ba", None),
        P("aa", None, None),
        P(),
        P(),
        P("aa", None, None, "ba"),
    )
    return jax.shard_map(
        per_device,
        mesh=mesh,
        in_specs=placed,
        out_specs=(P("aa", None, None, "ba"), P("aa", None, None, "ba", None)),
        check_vma=False,
    )
```

```python
import functools
import math

import jax
import jax.numpy as jnp
from jax import lax
from jax.experimental import pallas as pl
from jax.experimental.pallas import tpu as pltpu
from jax.sharding import PartitionSpec as P

TRUNCATION = 1279
FIELDS = 3
PAIRS = 80
WAVES = 1280
COLS = 164
OWNERS = 32
BROWS = 176
TAIL = COLS - 128
PAIR_BLOCK = 16
F32 = jnp.float32
BF16 = jnp.bfloat16
NT = (((1,), (1,)), ((), ()))
NN = (((1,), (0,)), ((), ()))


def vmem_params(mib):
    return pltpu.CompilerParams(vmem_limit_bytes=mib << 20)


def join_tails(first, second, third):
    return first + pltpu.roll(second, TAIL, axis=1) + pltpu.roll(third, 2 * TAIL, axis=1)


def tail_of(joined, field):
    return pltpu.roll(joined, 128 - TAIL * field, axis=1) if field else joined


def pack_kernel(x_ref, spec_ref, leg_ref, o_ref, spec_out, leg_out, held, arrived, rows, fetched):
    fetches = (
        pltpu.make_async_copy(spec_ref, spec_out, fetched.at[0]),
        pltpu.make_async_copy(leg_ref.at[pl.ds(0, PAIR_BLOCK)], leg_out, fetched.at[1]),
    )

    def part(k):
        return pltpu.make_async_copy(x_ref.at[pl.ds(6 * k, 6)], held.at[pl.ds(6 * k, 6)], arrived.at[k])

    for k in range(4):
        part(k).start()
    for fetch in fetches:
        fetch.start()
    for k in range(4):
        part(k).wait()
        for pair in (2 * k, 2 * k + 1):
            tails = []
            for f in range(FIELDS):
                x = held[3 * pair + f].astype(F32)
                rows[k, pl.ds(pair % 2 * 3 + f, OWNERS, stride=8), :] = x[:, 0:128]
                tails.append(jnp.concatenate([x[:, 128:COLS], jnp.zeros((OWNERS, 128 - TAIL), F32)], axis=1))
            rows[k, pl.ds(6 + pair % 2, OWNERS, stride=8), :] = join_tails(*tails)
        o_ref[:, 8 * k : 8 * k + 8, :] = rows[k].reshape(OWNERS, 8, 128).astype(BF16)
    for fetch in fetches:
        fetch.wait()


def pack_rows(x, spec, legendre):
    slots = legendre.shape[2]
    return pl.pallas_call(
        pack_kernel,
        in_specs=[pl.BlockSpec(memory_space=pltpu.HBM)] * 3,
        out_specs=[pl.BlockSpec(memory_space=pltpu.VMEM)] * 3,
        out_shape=[
            jax.ShapeDtypeStruct((OWNERS, 32, 128), BF16),
            pltpu.VMEM((PAIRS, FIELDS, 2, slots), BF16),
            pltpu.VMEM((PAIR_BLOCK, 32, slots), BF16),
        ],
        scratch_shapes=[
            pltpu.VMEM((24, OWNERS, COLS), BF16),
            pltpu.SemaphoreType.DMA((4,)),
            pltpu.VMEM((4, OWNERS * 8, 128), F32),
            pltpu.SemaphoreType.DMA((2,)),
        ],
        compiler_params=vmem_params(4),
        cost_estimate=pl.CostEstimate(flops=0, bytes_accessed=800_000, transcendentals=0),
        name="pack_rows",
    )(pltpu.with_memory_space_constraint(x, pltpu.HBM), spec, legendre)


def unpack_kernel(x_ref, o_ref, rows, held, written):
    copies = []
    for lat in range(4):
        rows[lat] = x_ref[:, 8 * lat : 8 * lat + 8, :].astype(F32).reshape(OWNERS * 8, 128)
        for h in range(2):
            joined = rows[lat, pl.ds(6 + h, OWNERS, stride=8), :]
            for f in range(FIELDS):
                own = rows[lat, pl.ds(3 * h + f, OWNERS, stride=8), :]
                held[6 * lat + 3 * h + f, :, 0:128] = own.astype(BF16)
                held[6 * lat + 3 * h + f, :, 128:COLS] = tail_of(joined, f)[:, 0:TAIL].astype(BF16)
        part = pl.ds(6 * lat, 6)
        copies.append(pltpu.make_async_copy(held.at[part], o_ref.at[part], written.at[lat]))
        copies[lat].start()
    for copy in copies:
        copy.wait()


def unpack_rows(x):
    return pl.pallas_call(
        unpack_kernel,
        in_specs=[pl.BlockSpec(memory_space=pltpu.VMEM)],
        out_specs=pl.BlockSpec(memory_space=pltpu.HBM),
        out_shape=pltpu.HBM((24, OWNERS, COLS), BF16),
        scratch_shapes=[
            pltpu.VMEM((4, OWNERS * 8, 128), F32),
            pltpu.VMEM((24, OWNERS, COLS), BF16),
            pltpu.SemaphoreType.DMA((4,)),
        ],
        compiler_params=vmem_params(4),
        cost_estimate=pl.CostEstimate(flops=0, bytes_accessed=800_000, transcendentals=0),
        name="unpack_rows",
    )(x)


def legendre_block(leg_ref, held, arrived, k):
    rows = pl.ds(pl.multiple_of(k * PAIR_BLOCK, PAIR_BLOCK), PAIR_BLOCK)
    return pltpu.make_async_copy(leg_ref.at[rows], held.at[rows], arrived.at[k])


def legendre_start(leg_ref, held, arrived):
    for k in range(1, PAIRS // PAIR_BLOCK):
        legendre_block(leg_ref, held, arrived, k).start()


def legendre_inverse_kernel(
    pw_ref, me_ref, leg_ref, block_ref, spec_ref, out_ref, held, arrived, by_pair, by_lat
):
    step = pl.program_id(0)
    slots = leg_ref.shape[2]
    slot = lax.broadcasted_iota(jnp.int32, (8, slots), 1)
    alternate = jnp.where(slot % 2 == 0, 1.0, -1.0).astype(F32)
    valid = slot <= TRUNCATION + 1
    row = lax.broadcasted_iota(jnp.int32, (32, 32), 0)

    def sum_block(table):
        for k in range(PAIR_BLOCK):
            pair = step * PAIR_BLOCK + k
            wave = pw_ref[me_ref[0] * PAIRS + pair]
            first = slot <= TRUNCATION - wave
            a = jnp.concatenate(
                [spec_ref[pair, f].astype(F32) for f in range(FIELDS)] + [jnp.zeros((2, slots), F32)], axis=0
            )
            a = jnp.where(valid, a, 0.0)
            b = a * alternate
            lhs = jnp.concatenate(
                [
                    jnp.where(first, a, 0.0),
                    jnp.where(first, b, 0.0),
                    jnp.where(first, 0.0, a),
                    jnp.where(first, 0.0, b),
                ],
                axis=0,
            ).astype(BF16)
            sums = lax.dot_general(lhs, table(k), NT, preferred_element_type=F32)
            sign = (1 - 2 * (wave % 2)).astype(F32)
            sums = jnp.where(row >= 24, sums * sign, sums)
            by_pair[pl.ds(pair, 32, stride=PAIRS), :] = jnp.concatenate(
                [sums, jnp.zeros((32, 96), F32)], axis=1
            )

    @pl.when(step == 0)
    def _():
        legendre_start(leg_ref, held, arrived)
        sum_block(lambda k: block_ref[k])

    @pl.when(step > 0)
    def _():
        legendre_block(leg_ref, held, arrived, step).wait()
        sum_block(lambda k: held[step * PAIR_BLOCK + k])

    @pl.when(step == pl.num_programs(0) - 1)
    def _():
        for half in range(4):
            h, w = half % 2, half // 2
            for c in range(6):
                start = (half * 8 + c) * PAIRS
                turned = jnp.concatenate(
                    [by_pair[start : start + PAIRS, :], jnp.zeros((48, 128), F32)], axis=0
                ).T
                by_lat[w, pl.ds(h * 6 + (c % 2) * 3 + c // 2, 32, stride=12), :] = turned[0:32, :]
        x, core = me_ref[0] // 2, me_ref[0] % 2
        for s in range(4):
            for d in range(2):
                dest = ((x + s) % 4) * 2 + (core + d) % 2
                rows = pl.ds(pl.multiple_of(dest * 48, 8), 48)
                out_ref[s, d, :, 0:128] = by_lat[0, rows, :].astype(BF16)
                out_ref[s, d, :, 128:256] = by_lat[1, rows, :].astype(BF16)


def legendre_inverse(pair_wave, me, legendre, block, spec):
    slots = legendre.shape[2]
    return pl.pallas_call(
        legendre_inverse_kernel,
        grid_spec=pltpu.PrefetchScalarGridSpec(
            num_scalar_prefetch=2,
            grid=(PAIRS // PAIR_BLOCK,),
            in_specs=[
                pl.BlockSpec(memory_space=pltpu.HBM),
                pl.BlockSpec(memory_space=pltpu.VMEM),
                pl.BlockSpec(memory_space=pltpu.VMEM),
            ],
            out_specs=pl.BlockSpec((4, 2, 48, 256), lambda i, *_: (0, 0, 0, 0)),
            scratch_shapes=[
                pltpu.VMEM((PAIRS, 32, slots), BF16),
                pltpu.SemaphoreType.DMA((PAIRS // PAIR_BLOCK,)),
                pltpu.VMEM((32 * PAIRS, 128), F32),
                pltpu.VMEM((2, 384, 128), F32),
            ],
        ),
        out_shape=jax.ShapeDtypeStruct((4, 2, 48, 256), BF16),
        compiler_params=vmem_params(16),
        cost_estimate=pl.CostEstimate(flops=2 * 80 * 32 * 32 * 1288, bytes_accessed=9_000_000, transcendentals=0),
        name="legendre_inverse",
    )(pair_wave, me, legendre, block, spec)


def join_pieces(pieces):
    lane = lax.broadcasted_iota(jnp.int32, pieces[0].shape, 1)
    rolled = [pltpu.roll(p, (80 * i) % 128, axis=1) if (80 * i) % 128 else p for i, p in enumerate(pieces)]
    tiles = []
    for k in range(10):
        tile = None
        for i in range(16):
            low, high = 80 * i - 128 * k, 80 * i + 80 - 128 * k
            if high <= 0 or low >= 128:
                continue
            tile = rolled[i] if tile is None else jnp.where(lane >= low, rolled[i], tile)
        tiles.append(tile)
    return tiles


def cut_piece(ref, i):
    tile, shift = (80 * i) // 128, (80 * i) % 128
    low = ref[:, tile * 128 : tile * 128 + 128]
    if shift == 0:
        return low
    low = pltpu.roll(low, 128 - shift, axis=1)
    if shift + 80 <= 128:
        return low
    high = pltpu.roll(ref[:, tile * 128 + 128 : tile * 128 + 256], 128 - shift, axis=1)
    lane = lax.broadcasted_iota(jnp.int32, low.shape, 1)
    return jnp.where(lane < 128 - shift, low, high)


def cos_sin(turn, length):
    times = jnp.floor(turn * (1.0 / length) + 0.5)
    u = (turn - times * length) * (math.pi / length)
    u2 = u * u
    s = u * (
        1.0
        + u2
        * (
            -1.0 / 6
            + u2 * (1.0 / 120 + u2 * (-1.0 / 5040 + u2 * (1.0 / 362880 + u2 * (-1.0 / 39916800))))
        )
    )
    c = 1.0 + u2 * (
        -0.5
        + u2
        * (
            1.0 / 24
            + u2
            * (-1.0 / 720 + u2 * (1.0 / 40320 + u2 * (-1.0 / 3628800 + u2 * (1.0 / 479001600))))
        )
    )
    return 1.0 - 2.0 * s * s, 2.0 * s * c


def table_kernel(me_ref, waves_ref, outer_ref, inner_ref, factor_ref, wave_row):
    lat = pl.program_id(0)
    me = me_ref[0]
    x, core = me // 2, me % 2

    @pl.when(lat == 0)
    def _():
        pieces = []
        for d in range(2):
            for s in range(4):
                source = ((x + 4 - s) % 4) * 2 + (core + d) % 2
                for w in range(2):
                    pieces.append(jnp.broadcast_to(waves_ref[source, w : w + 1, :], (8, 128)))
        for k, tile in enumerate(join_pieces(pieces)):
            wave_row[:, 128 * k : 128 * k + 128] = tile
            factor_ref[:, 128 * k : 128 * k + 128] = jnp.where(tile == 0.0, 1.0, 2.0)

    length = jnp.full((1, 1), (5012 + 16 * me + 4 * lat).astype(F32), F32)
    wave = wave_row[...]
    eight = lax.broadcasted_iota(jnp.int32, (8, WAVES), 0).astype(F32)
    low_c, low_s = cos_sin(wave * (eight * COLS), length)
    single = lax.broadcasted_iota(jnp.int32, (8, WAVES), 0)
    steps = jnp.where(single < 4, single * (8 * COLS), (single - 4) * 64).astype(F32)
    step_c, step_s = cos_sin(wave * steps, length)
    high_c, high_s = step_c, step_s
    for k in range(4):
        hc, hs = high_c[k : k + 1, :], high_s[k : k + 1, :]
        outer_ref[0, 0, 8 * k : 8 * k + 8, :] = low_c * hc - low_s * hs
        outer_ref[0, 1, 8 * k : 8 * k + 8, :] = low_s * hc + low_c * hs
    low_c, low_s = cos_sin(wave * eight, length)
    first_c, first_s = cos_sin(wave * (eight * 8.0), length)
    for block in range(3):
        high_c, high_s = first_c, first_s
        if block:
            sc, ss = step_c[4 + block : 5 + block, :], step_s[4 + block : 5 + block, :]
            high_c, high_s = first_c * sc - first_s * ss, first_s * sc + first_c * ss
        for k in range(0, 8, 2):
            base = 64 * block + 8 * k
            if base >= BROWS:
                continue
            parts_c, parts_s = [], []
            for kk in (k, k + 1):
                hc, hs = high_c[kk : kk + 1, :], high_s[kk : kk + 1, :]
                parts_c.append(low_c * hc - low_s * hs)
                parts_s.append(low_s * hc + low_c * hs)
            inner_ref[0, base : base + 16, 0:WAVES] = jnp.concatenate(parts_c, axis=0).astype(BF16)
            inner_ref[0, base : base + 16, WAVES:] = jnp.concatenate(parts_s, axis=0).astype(BF16)


def phase_tables(me, waves):
    return pl.pallas_call(
        table_kernel,
        grid_spec=pltpu.PrefetchScalarGridSpec(
            num_scalar_prefetch=1,
            grid=(4,),
            in_specs=[pl.BlockSpec((8, 2, 128), lambda i, *_: (0, 0, 0))],
            out_specs=[
                pl.BlockSpec((1, 2, OWNERS, WAVES), lambda i, *_: (i, 0, 0, 0)),
                pl.BlockSpec((1, BROWS, 2 * WAVES), lambda i, *_: (i, 0, 0)),
                pl.BlockSpec((8, WAVES), lambda i, *_: (0, 0)),
            ],
            scratch_shapes=[pltpu.VMEM((8, WAVES), F32)],
        ),
        out_shape=[
            jax.ShapeDtypeStruct((4, 2, OWNERS, WAVES), F32),
            jax.ShapeDtypeStruct((4, BROWS, 2 * WAVES), BF16),
            jax.ShapeDtypeStruct((8, WAVES), F32),
        ],
        compiler_params=vmem_params(8),
        cost_estimate=pl.CostEstimate(flops=40_000_000, bytes_accessed=5_000_000, transcendentals=0),
        name="phase_tables",
    )(me, waves)


def inside_mask(me, lat):
    length = 5012 + 16 * me + 4 * lat
    owner = lax.broadcasted_iota(jnp.int32, (OWNERS, BROWS), 0)
    col = lax.broadcasted_iota(jnp.int32, (OWNERS, BROWS), 1)
    return (col < COLS) & (owner * COLS + col < length)


def row_kernel(
    me_ref,
    weight_ref,
    kept_ref,
    got_ref,
    forcing_ref,
    outer_ref,
    inner_ref,
    factor_ref,
    leg_ref,
    send_ref,
    own_ref,
    other_ref,
    block_ref,
    fetched,
    coeffs,
    turned,
    grid_rows,
    force_rows,
    values,
    samples,
    sums,
):
    lat = pl.program_id(0)
    me = me_ref[0]

    fetch = pltpu.make_async_copy(leg_ref.at[pl.ds(0, PAIR_BLOCK)], block_ref, fetched)

    @pl.when(lat == 0)
    def _():
        fetch.start()
        pieces = []
        for ref in (kept_ref, got_ref):
            for s in range(4):
                for w in range(2):
                    pieces.append(ref[s, :, 128 * w : 128 * w + 128].astype(F32))
        for k, tile in enumerate(join_pieces(pieces)):
            coeffs[:, 128 * k : 128 * k + 128] = tile * factor_ref[0:1, 128 * k : 128 * k + 128]
        for j in range(OWNERS):
            force_rows[32 * j : 32 * j + 32, :] = forcing_ref[j].astype(F32)

    for r in range(6):
        h, f = r // 3, r % 3
        real = coeffs[pl.ds(lat * 12 + h * 6 + f, 1), :]
        imag = coeffs[pl.ds(lat * 12 + h * 6 + 3 + f, 1), :]
        oc, os = outer_ref[lat, 0], outer_ref[lat, 1]
        turned[32 * r : 32 * r + 32, 0:WAVES] = (real * oc - imag * os).astype(BF16)
        turned[32 * r : 32 * r + 32, WAVES:] = (-(real * os + imag * oc)).astype(BF16)
    rows = lax.dot_general(turned[...], inner_ref[lat], NT, preferred_element_type=F32)
    inside = inside_mask(me, lat)
    for r in range(6):
        value = jnp.where(inside, rows[32 * r : 32 * r + 32, :], 0.0).astype(BF16).astype(F32)
        values[32 * r : 32 * r + 32, :] = value
        grid_rows[pl.ds(r, OWNERS, stride=8), :] = value[:, 0:128]
    for h in range(2):
        tails = [
            jnp.concatenate(
                [values[32 * r : 32 * r + 32, 128:BROWS], jnp.zeros((OWNERS, 256 - BROWS), F32)], axis=1
            )
            for r in range(3 * h, 3 * h + 3)
        ]
        grid_rows[pl.ds(6 + h, OWNERS, stride=8), :] = join_tails(*tails)
    send_ref[...] = grid_rows[...].reshape(OWNERS, 8, 128).astype(BF16)
    for r in range(6):
        h, f = r // 3, r % 3
        other = h * 3 + (f + 1) % 3
        product = values[32 * r : 32 * r + 32, :] * values[32 * other : 32 * other + 32, :]
        tail = tail_of(force_rows[pl.ds(lat * 8 + 6 + h, OWNERS, stride=32), :], f)
        force = jnp.concatenate(
            [force_rows[pl.ds(lat * 8 + r, OWNERS, stride=32), :], tail[:, 0 : BROWS - 128]], axis=1
        )
        samples[32 * r : 32 * r + 32, :] = jnp.where(inside, product + force, 0.0).astype(BF16)
    length = jnp.full((1, 256), (5012 + 16 * me + 4 * lat).astype(F32), F32)
    scale = weight_ref[me * 4 + lat] * lax.rsqrt(length)
    data = samples[...]
    for n in range(0, WAVES, 256):
        part_c = lax.dot_general(data, inner_ref[lat, :, n : n + 256], NN, preferred_element_type=F32)
        part_s = lax.dot_general(
            data, inner_ref[lat, :, WAVES + n : WAVES + n + 256], NN, preferred_element_type=F32
        )
        oc, os = outer_ref[lat, 0, :, n : n + 256], outer_ref[lat, 1, :, n : n + 256]
        for r in range(6):
            h, f = r // 3, r % 3
            pc, ps = part_c[32 * r : 32 * r + 32, :], part_s[32 * r : 32 * r + 32, :]
            real = jnp.sum(pc * oc - ps * os, axis=0, keepdims=True)
            imag = jnp.sum(ps * oc + pc * os, axis=0, keepdims=True)
            sums[pl.ds(lat * 12 + h * 6 + f, 1), n : n + 256] = real * scale
            sums[pl.ds(lat * 12 + h * 6 + 3 + f, 1), n : n + 256] = -imag * scale

    @pl.when(lat == 3)
    def _():
        for d, ref in enumerate((own_ref, other_ref)):
            for s in range(4):
                for w in range(2):
                    piece = cut_piece(sums, (d * 4 + s) * 2 + w)
                    ref[s, :, 128 * w : 128 * w + 128] = piece.astype(BF16)
        fetch.wait()


def transform_rows(me, weight, kept, got, forcing, outer, inner, factor, legendre):
    slots = legendre.shape[2]
    return pl.pallas_call(
        row_kernel,
        grid_spec=pltpu.PrefetchScalarGridSpec(
            num_scalar_prefetch=2,
            grid=(4,),
            in_specs=[
                pl.BlockSpec((4, 48, 256), lambda i, *_: (0, 0, 0)),
                pl.BlockSpec((4, 48, 256), lambda i, *_: (0, 0, 0)),
                pl.BlockSpec(memory_space=pltpu.VMEM),
                pl.BlockSpec(memory_space=pltpu.VMEM),
                pl.BlockSpec(memory_space=pltpu.VMEM),
                pl.BlockSpec(memory_space=pltpu.VMEM),
                pl.BlockSpec(memory_space=pltpu.HBM),
            ],
            out_specs=[
                pl.BlockSpec((OWNERS, 8, 128), lambda i, *_: (0, i, 0)),
                pl.BlockSpec((4, 48, 256), lambda i, *_: (0, 0, 0)),
                pl.BlockSpec((4, 48, 256), lambda i, *_: (0, 0, 0)),
                pl.BlockSpec(memory_space=pltpu.VMEM),
            ],
            scratch_shapes=[
                pltpu.SemaphoreType.DMA,
                pltpu.VMEM((48, WAVES), F32),
                pltpu.VMEM((192, 2 * WAVES), BF16),
                pltpu.VMEM((OWNERS * 8, 128), F32),
                pltpu.VMEM((1024, 128), F32),
                pltpu.VMEM((192, BROWS), F32),
                pltpu.VMEM((192, BROWS), BF16),
                pltpu.VMEM((48, WAVES), F32),
            ],
        ),
        out_shape=[
            pltpu.HBM((OWNERS, 32, 128), BF16),
            jax.ShapeDtypeStruct((4, 48, 256), BF16),
            jax.ShapeDtypeStruct((4, 48, 256), BF16),
            pltpu.VMEM((PAIR_BLOCK, 32, slots), BF16),
        ],
        compiler_params=vmem_params(14),
        cost_estimate=pl.CostEstimate(flops=1_400_000_000, bytes_accessed=6_000_000, transcendentals=0),
        name="transform_rows",
    )(
        me,
        weight,
        kept,
        got,
        forcing,
        outer,
        inner,
        factor,
        legendre,
    )


def legendre_direct_kernel(
    pw_ref, me_ref, first_ref, second_ref, third_ref, fourth_ref, leg_ref, block_ref, out_ref, held, arrived, by_lat, by_pair
):
    step = pl.program_id(0)
    slots = leg_ref.shape[2]

    @pl.when(step == 0)
    def _():
        legendre_start(leg_ref, held, arrived)
        x, core = me_ref[0] // 2, me_ref[0] % 2
        for s, ref in enumerate((first_ref, second_ref, third_ref, fourth_ref)):
            for d in range(2):
                source = ((x + s) % 4) * 2 + (core + d) % 2
                rows = pl.ds(pl.multiple_of(source * 48, 8), 48)
                for w in range(2):
                    by_lat[w, rows, :] = ref[d, :, 128 * w : 128 * w + 128].astype(F32)
        for w in range(2):
            for c in range(6):
                north = by_lat[w, pl.ds(c, 32, stride=12), :]
                south = by_lat[w, pl.ds(6 + c, 32, stride=12), :]
                for odd, value in enumerate((north + south, north - south)):
                    turned = jnp.concatenate([value, jnp.zeros((96, 128), F32)], axis=0).T
                    row = (w * 2 + odd) * 8 + (c % 3) * 2 + c // 3
                    by_pair[pl.ds(row, PAIRS, stride=32), :] = turned[0:PAIRS, :]

    slot = lax.broadcasted_iota(jnp.int32, (8, slots), 1)
    even = slot % 2 == 0
    valid = slot <= TRUNCATION + 1

    def sum_block(table):
        for k in range(PAIR_BLOCK):
            pair = step * PAIR_BLOCK + k
            wave = pw_ref[me_ref[0] * PAIRS + pair]
            lhs = by_pair[pl.ds(pl.multiple_of(pair * 32, 32), 32), :][:, 0:32].astype(BF16)
            sums = lax.dot_general(lhs, table(k), NN, preferred_element_type=F32)
            first = jnp.where(even, sums[0:8], sums[8:16])
            second = jnp.where((slot + wave) % 2 == 0, sums[16:24], sums[24:32])
            value = jnp.where(slot <= TRUNCATION - wave, first, second)
            value = jnp.where(valid, value, 0.0).astype(BF16)
            for f in range(FIELDS):
                out_ref[k, f] = value[2 * f : 2 * f + 2]

    @pl.when(step == 0)
    def _():
        sum_block(lambda k: block_ref[k])

    @pl.when(step > 0)
    def _():
        legendre_block(leg_ref, held, arrived, step).wait()
        sum_block(lambda k: held[step * PAIR_BLOCK + k])


def legendre_direct(pair_wave, me, came, legendre, block):
    slots = legendre.shape[2]
    return pl.pallas_call(
        legendre_direct_kernel,
        grid_spec=pltpu.PrefetchScalarGridSpec(
            num_scalar_prefetch=2,
            grid=(PAIRS // PAIR_BLOCK,),
            in_specs=[pl.BlockSpec((2, 48, 256), lambda i, *_: (0, 0, 0))] * 4
            + [pl.BlockSpec(memory_space=pltpu.HBM), pl.BlockSpec(memory_space=pltpu.VMEM)],
            out_specs=pl.BlockSpec((PAIR_BLOCK, FIELDS, 2, slots), lambda i, *_: (i, 0, 0, 0)),
            scratch_shapes=[
                pltpu.VMEM((PAIRS, 32, slots), BF16),
                pltpu.SemaphoreType.DMA((PAIRS // PAIR_BLOCK,)),
                pltpu.VMEM((2, 384, 128), F32),
                pltpu.VMEM((32 * PAIRS, 128), F32),
            ],
        ),
        out_shape=jax.ShapeDtypeStruct((PAIRS, FIELDS, 2, slots), BF16),
        compiler_params=vmem_params(16),
        cost_estimate=pl.CostEstimate(flops=2 * 80 * 32 * 32 * 1288, bytes_accessed=9_000_000, transcendentals=0),
        name="legendre_direct",
    )(pair_wave, me, *came, legendre, block)


def to_chip(value, distance):
    return lax.ppermute(value, "aa", [(i, ((i // 2 + distance) % 4) * 2 + i % 2) for i in range(8)])


def to_other_core(value):
    return lax.ppermute(value, "aa", [(i, i ^ 1) for i in range(8)])


def per_device(spec_in, legendre, pair_wave, quad_weight, forcing):
    me = lax.axis_index("aa").astype(jnp.int32).reshape(1)
    legendre = pltpu.with_memory_space_constraint(legendre, pltpu.HBM)
    wave_table = pltpu.with_memory_space_constraint(pair_wave, pltpu.HBM)
    spec = jnp.swapaxes(spec_in.reshape(PAIRS, 2, FIELDS, -1), 1, 2)
    spec = pltpu.with_memory_space_constraint(spec, pltpu.HBM)
    forcing_send, spec, block = pack_rows(forcing.reshape(24, OWNERS, COLS), spec, legendre)
    forcing_here = lax.all_to_all(forcing_send, "ba", split_axis=0, concat_axis=0, tiled=True)
    fourier = legendre_inverse(wave_table, me, legendre, block, spec)
    pairs = pair_wave.astype(F32).reshape(8, PAIRS)
    waves = jnp.pad(jnp.stack([pairs, TRUNCATION - pairs], axis=1), ((0, 0), (0, 0), (0, 48)))
    waves, forcing_here = lax.optimization_barrier((waves, forcing_here))
    outer, inner, factor = phase_tables(me, waves)
    came = [fourier[0]] + [to_chip(fourier[s], s) for s in range(1, 4)]
    *came, factor = lax.optimization_barrier((*came, factor))
    kept = jnp.stack([c[0] for c in came])
    got = to_other_core(jnp.stack([c[1] for c in came]))
    grid_send, own, other, block = transform_rows(
        me, quad_weight, kept, got, forcing_here, outer, inner, factor, legendre
    )
    staying, grid_send = lax.optimization_barrier((own[0], grid_send))
    grid_came = lax.all_to_all(grid_send, "ba", split_axis=0, concat_axis=0, tiled=True)
    passed = to_other_core(other)
    parts = [jnp.stack([own[s] if s else staying, passed[s]]) for s in range(4)]
    came = [parts[0]] + [to_chip(parts[s], -s) for s in range(1, 4)]
    spec_out = legendre_direct(wave_table, me, came, legendre, block)
    grid = unpack_rows(grid_came)
    return (
        grid.reshape(8, FIELDS, OWNERS, COLS),
        jnp.swapaxes(spec_out, 1, 2).reshape(PAIRS, 2, FIELDS, 1, -1),
    )


def solution(mesh):
    placed = (
        P("aa", None, None, "ba", None),
        P("aa", None, None),
        P(),
        P(),
        P("aa", None, None, "ba"),
    )
    return jax.shard_map(
        per_device,
        mesh=mesh,
        in_specs=placed,
        out_specs=(P("aa", None, None, "ba"), P("aa", None, None, "ba", None)),
        check_vma=False,
    )
```

```python
import functools
import math

import jax
import jax.numpy as jnp
from jax import lax
from jax.experimental import pallas as pl
from jax.experimental.pallas import tpu as pltpu
from jax.sharding import PartitionSpec as P

TRUNCATION = 1279
FIELDS = 3
PAIRS = 80
WAVES = 1280
COLS = 164
OWNERS = 32
BROWS = 176
TAIL = COLS - 128
PAIR_BLOCK = 16
F32 = jnp.float32
BF16 = jnp.bfloat16
NT = (((1,), (1,)), ((), ()))
NN = (((1,), (0,)), ((), ()))


def vmem_params(mib):
    return pltpu.CompilerParams(vmem_limit_bytes=mib << 20)


def join_tails(first, second, third):
    return first + pltpu.roll(second, TAIL, axis=1) + pltpu.roll(third, 2 * TAIL, axis=1)


def tail_of(joined, field):
    return pltpu.roll(joined, 128 - TAIL * field, axis=1) if field else joined


def pack_kernel(x_ref, spec_ref, o_ref, spec_out, held, arrived, rows, fetched):
    fetch = pltpu.make_async_copy(spec_ref, spec_out, fetched)

    def part(k):
        return pltpu.make_async_copy(x_ref.at[pl.ds(6 * k, 6)], held.at[pl.ds(6 * k, 6)], arrived.at[k])

    for k in range(4):
        part(k).start()
    fetch.start()
    for k in range(4):
        part(k).wait()
        for pair in (2 * k, 2 * k + 1):
            tails = []
            for f in range(FIELDS):
                x = held[3 * pair + f].astype(F32)
                rows[k, pl.ds(pair % 2 * 3 + f, OWNERS, stride=8), :] = x[:, 0:128]
                tails.append(jnp.concatenate([x[:, 128:COLS], jnp.zeros((OWNERS, 128 - TAIL), F32)], axis=1))
            rows[k, pl.ds(6 + pair % 2, OWNERS, stride=8), :] = join_tails(*tails)
        o_ref[:, 8 * k : 8 * k + 8, :] = rows[k].reshape(OWNERS, 8, 128).astype(BF16)
    fetch.wait()


def pack_rows(x, spec):
    slots = spec.shape[3]
    return pl.pallas_call(
        pack_kernel,
        in_specs=[pl.BlockSpec(memory_space=pltpu.HBM)] * 2,
        out_specs=[pl.BlockSpec(memory_space=pltpu.VMEM)] * 2,
        out_shape=[
            jax.ShapeDtypeStruct((OWNERS, 32, 128), BF16),
            pltpu.VMEM((PAIRS, FIELDS, 2, slots), BF16),
        ],
        scratch_shapes=[
            pltpu.VMEM((24, OWNERS, COLS), BF16),
            pltpu.SemaphoreType.DMA((4,)),
            pltpu.VMEM((4, OWNERS * 8, 128), F32),
            pltpu.SemaphoreType.DMA,
        ],
        compiler_params=vmem_params(4),
        cost_estimate=pl.CostEstimate(flops=0, bytes_accessed=800_000, transcendentals=0),
        name="pack_rows",
    )(pltpu.with_memory_space_constraint(x, pltpu.HBM), spec)


def unpack_kernel(x_ref, o_ref, rows, held, written):
    copies = []
    for lat in range(4):
        rows[lat] = x_ref[:, 8 * lat : 8 * lat + 8, :].astype(F32).reshape(OWNERS * 8, 128)
        for h in range(2):
            joined = rows[lat, pl.ds(6 + h, OWNERS, stride=8), :]
            for f in range(FIELDS):
                own = rows[lat, pl.ds(3 * h + f, OWNERS, stride=8), :]
                held[6 * lat + 3 * h + f, :, 0:128] = own.astype(BF16)
                held[6 * lat + 3 * h + f, :, 128:COLS] = tail_of(joined, f)[:, 0:TAIL].astype(BF16)
        part = pl.ds(6 * lat, 6)
        copies.append(pltpu.make_async_copy(held.at[part], o_ref.at[part], written.at[lat]))
        copies[lat].start()
    for copy in copies:
        copy.wait()


def unpack_rows(x):
    return pl.pallas_call(
        unpack_kernel,
        in_specs=[pl.BlockSpec(memory_space=pltpu.VMEM)],
        out_specs=pl.BlockSpec(memory_space=pltpu.HBM),
        out_shape=pltpu.HBM((24, OWNERS, COLS), BF16),
        scratch_shapes=[
            pltpu.VMEM((4, OWNERS * 8, 128), F32),
            pltpu.VMEM((24, OWNERS, COLS), BF16),
            pltpu.SemaphoreType.DMA((4,)),
        ],
        compiler_params=vmem_params(4),
        cost_estimate=pl.CostEstimate(flops=0, bytes_accessed=800_000, transcendentals=0),
        name="unpack_rows",
    )(x)


def legendre_block(leg_ref, held, arrived, k):
    rows = pl.ds(pl.multiple_of(k * PAIR_BLOCK, PAIR_BLOCK), PAIR_BLOCK)
    return pltpu.make_async_copy(leg_ref.at[rows], held.at[rows], arrived.at[k])


def legendre_start(leg_ref, held, arrived, first):
    for k in range(first, PAIRS // PAIR_BLOCK):
        legendre_block(leg_ref, held, arrived, k).start()


def legendre_inverse_kernel(
    pw_ref, me_ref, leg_ref, spec_ref, out_ref, held, arrived, by_pair, by_lat
):
    step = pl.program_id(0)
    slots = leg_ref.shape[2]
    slot = lax.broadcasted_iota(jnp.int32, (8, slots), 1)
    alternate = jnp.where(slot % 2 == 0, 1.0, -1.0).astype(F32)
    valid = slot <= TRUNCATION + 1
    row = lax.broadcasted_iota(jnp.int32, (32, 32), 0)

    def sum_block(table):
        for k in range(PAIR_BLOCK):
            pair = step * PAIR_BLOCK + k
            wave = pw_ref[me_ref[0] * PAIRS + pair]
            first = slot <= TRUNCATION - wave
            a = jnp.concatenate(
                [spec_ref[pair, f].astype(F32) for f in range(FIELDS)] + [jnp.zeros((2, slots), F32)], axis=0
            )
            a = jnp.where(valid, a, 0.0)
            b = a * alternate
            lhs = jnp.concatenate(
                [
                    jnp.where(first, a, 0.0),
                    jnp.where(first, b, 0.0),
                    jnp.where(first, 0.0, a),
                    jnp.where(first, 0.0, b),
                ],
                axis=0,
            ).astype(BF16)
            sums = lax.dot_general(lhs, table(k), NT, preferred_element_type=F32)
            sign = (1 - 2 * (wave % 2)).astype(F32)
            sums = jnp.where(row >= 24, sums * sign, sums)
            by_pair[pl.ds(pair, 32, stride=PAIRS), :] = jnp.concatenate(
                [sums, jnp.zeros((32, 96), F32)], axis=1
            )

    @pl.when(step == 0)
    def _():
        legendre_start(leg_ref, held, arrived, 0)

    legendre_block(leg_ref, held, arrived, step).wait()
    sum_block(lambda k: held[step * PAIR_BLOCK + k])

    @pl.when(step == pl.num_programs(0) - 1)
    def _():
        for half in range(4):
            h, w = half % 2, half // 2
            for c in range(6):
                start = (half * 8 + c) * PAIRS
                turned = jnp.concatenate(
                    [by_pair[start : start + PAIRS, :], jnp.zeros((48, 128), F32)], axis=0
                ).T
                by_lat[w, pl.ds(h * 6 + (c % 2) * 3 + c // 2, 32, stride=12), :] = turned[0:32, :]
        x, core = me_ref[0] // 2, me_ref[0] % 2
        for s in range(4):
            for d in range(2):
                dest = ((x + s) % 4) * 2 + (core + d) % 2
                rows = pl.ds(pl.multiple_of(dest * 48, 8), 48)
                out_ref[s, d, :, 0:128] = by_lat[0, rows, :].astype(BF16)
                out_ref[s, d, :, 128:256] = by_lat[1, rows, :].astype(BF16)


def legendre_inverse(pair_wave, me, legendre, spec):
    slots = legendre.shape[2]
    return pl.pallas_call(
        legendre_inverse_kernel,
        grid_spec=pltpu.PrefetchScalarGridSpec(
            num_scalar_prefetch=2,
            grid=(PAIRS // PAIR_BLOCK,),
            in_specs=[
                pl.BlockSpec(memory_space=pltpu.HBM),
                pl.BlockSpec(memory_space=pltpu.VMEM),
            ],
            out_specs=pl.BlockSpec((4, 2, 48, 256), lambda i, *_: (0, 0, 0, 0)),
            scratch_shapes=[
                pltpu.VMEM((PAIRS, 32, slots), BF16),
                pltpu.SemaphoreType.DMA((PAIRS // PAIR_BLOCK,)),
                pltpu.VMEM((32 * PAIRS, 128), F32),
                pltpu.VMEM((2, 384, 128), F32),
            ],
        ),
        out_shape=jax.ShapeDtypeStruct((4, 2, 48, 256), BF16),
        compiler_params=vmem_params(16),
        cost_estimate=pl.CostEstimate(flops=2 * 80 * 32 * 32 * 1288, bytes_accessed=9_000_000, transcendentals=0),
        name="legendre_inverse",
    )(pair_wave, me, legendre, spec)


def join_pieces(pieces):
    lane = lax.broadcasted_iota(jnp.int32, pieces[0].shape, 1)
    rolled = [pltpu.roll(p, (80 * i) % 128, axis=1) if (80 * i) % 128 else p for i, p in enumerate(pieces)]
    tiles = []
    for k in range(10):
        tile = None
        for i in range(16):
            low, high = 80 * i - 128 * k, 80 * i + 80 - 128 * k
            if high <= 0 or low >= 128:
                continue
            tile = rolled[i] if tile is None else jnp.where(lane >= low, rolled[i], tile)
        tiles.append(tile)
    return tiles


def cut_piece(ref, i):
    tile, shift = (80 * i) // 128, (80 * i) % 128
    low = ref[:, tile * 128 : tile * 128 + 128]
    if shift == 0:
        return low
    low = pltpu.roll(low, 128 - shift, axis=1)
    if shift + 80 <= 128:
        return low
    high = pltpu.roll(ref[:, tile * 128 + 128 : tile * 128 + 256], 128 - shift, axis=1)
    lane = lax.broadcasted_iota(jnp.int32, low.shape, 1)
    return jnp.where(lane < 128 - shift, low, high)


def cos_sin(turn, length):
    times = jnp.floor(turn * (1.0 / length) + 0.5)
    u = (turn - times * length) * (math.pi / length)
    u2 = u * u
    s = u * (
        1.0
        + u2
        * (
            -1.0 / 6
            + u2 * (1.0 / 120 + u2 * (-1.0 / 5040 + u2 * (1.0 / 362880 + u2 * (-1.0 / 39916800))))
        )
    )
    c = 1.0 + u2 * (
        -0.5
        + u2
        * (
            1.0 / 24
            + u2
            * (-1.0 / 720 + u2 * (1.0 / 40320 + u2 * (-1.0 / 3628800 + u2 * (1.0 / 479001600))))
        )
    )
    return 1.0 - 2.0 * s * s, 2.0 * s * c


def table_kernel(me_ref, waves_ref, outer_ref, inner_ref, factor_ref, wave_row):
    lat = pl.program_id(0)
    me = me_ref[0]
    x, core = me // 2, me % 2

    @pl.when(lat == 0)
    def _():
        pieces = []
        for d in range(2):
            for s in range(4):
                source = ((x + 4 - s) % 4) * 2 + (core + d) % 2
                for w in range(2):
                    pieces.append(jnp.broadcast_to(waves_ref[source, w : w + 1, :], (8, 128)))
        for k, tile in enumerate(join_pieces(pieces)):
            wave_row[:, 128 * k : 128 * k + 128] = tile
            factor_ref[:, 128 * k : 128 * k + 128] = jnp.where(tile == 0.0, 1.0, 2.0)

    length = jnp.full((1, 1), (5012 + 16 * me + 4 * lat).astype(F32), F32)
    wave = wave_row[...]
    eight = lax.broadcasted_iota(jnp.int32, (8, WAVES), 0).astype(F32)
    low_c, low_s = cos_sin(wave * (eight * COLS), length)
    single = lax.broadcasted_iota(jnp.int32, (8, WAVES), 0)
    steps = jnp.where(single < 4, single * (8 * COLS), (single - 4) * 64).astype(F32)
    step_c, step_s = cos_sin(wave * steps, length)
    high_c, high_s = step_c, step_s
    for k in range(4):
        hc, hs = high_c[k : k + 1, :], high_s[k : k + 1, :]
        outer_ref[0, 0, 8 * k : 8 * k + 8, :] = low_c * hc - low_s * hs
        outer_ref[0, 1, 8 * k : 8 * k + 8, :] = low_s * hc + low_c * hs
    low_c, low_s = cos_sin(wave * eight, length)
    first_c, first_s = cos_sin(wave * (eight * 8.0), length)
    for block in range(3):
        high_c, high_s = first_c, first_s
        if block:
            sc, ss = step_c[4 + block : 5 + block, :], step_s[4 + block : 5 + block, :]
            high_c, high_s = first_c * sc - first_s * ss, first_s * sc + first_c * ss
        for k in range(0, 8, 2):
            base = 64 * block + 8 * k
            if base >= BROWS:
                continue
            parts_c, parts_s = [], []
            for kk in (k, k + 1):
                hc, hs = high_c[kk : kk + 1, :], high_s[kk : kk + 1, :]
                parts_c.append(low_c * hc - low_s * hs)
                parts_s.append(low_s * hc + low_c * hs)
            inner_ref[0, base : base + 16, 0:WAVES] = jnp.concatenate(parts_c, axis=0).astype(BF16)
            inner_ref[0, base : base + 16, WAVES:] = jnp.concatenate(parts_s, axis=0).astype(BF16)


def phase_tables(me, waves):
    return pl.pallas_call(
        table_kernel,
        grid_spec=pltpu.PrefetchScalarGridSpec(
            num_scalar_prefetch=1,
            grid=(4,),
            in_specs=[pl.BlockSpec((8, 2, 128), lambda i, *_: (0, 0, 0))],
            out_specs=[
                pl.BlockSpec((1, 2, OWNERS, WAVES), lambda i, *_: (i, 0, 0, 0)),
                pl.BlockSpec((1, BROWS, 2 * WAVES), lambda i, *_: (i, 0, 0)),
                pl.BlockSpec((8, WAVES), lambda i, *_: (0, 0)),
            ],
            scratch_shapes=[pltpu.VMEM((8, WAVES), F32)],
        ),
        out_shape=[
            jax.ShapeDtypeStruct((4, 2, OWNERS, WAVES), F32),
            jax.ShapeDtypeStruct((4, BROWS, 2 * WAVES), BF16),
            jax.ShapeDtypeStruct((8, WAVES), F32),
        ],
        compiler_params=vmem_params(8),
        cost_estimate=pl.CostEstimate(flops=40_000_000, bytes_accessed=5_000_000, transcendentals=0),
        name="phase_tables",
    )(me, waves)


def inside_mask(me, lat):
    length = 5012 + 16 * me + 4 * lat
    owner = lax.broadcasted_iota(jnp.int32, (OWNERS, BROWS), 0)
    col = lax.broadcasted_iota(jnp.int32, (OWNERS, BROWS), 1)
    return (col < COLS) & (owner * COLS + col < length)


def row_kernel(
    me_ref,
    weight_ref,
    kept_ref,
    got_ref,
    forcing_ref,
    outer_ref,
    inner_ref,
    factor_ref,
    leg_ref,
    send_ref,
    own_ref,
    other_ref,
    block_ref,
    fetched,
    coeffs,
    turned,
    grid_rows,
    force_rows,
    values,
    samples,
    sums,
):
    lat = pl.program_id(0)
    me = me_ref[0]

    fetch = pltpu.make_async_copy(leg_ref.at[pl.ds(0, PAIR_BLOCK)], block_ref, fetched)

    @pl.when(lat == 0)
    def _():
        fetch.start()
        pieces = []
        for ref in (kept_ref, got_ref):
            for s in range(4):
                for w in range(2):
                    pieces.append(ref[s, :, 128 * w : 128 * w + 128].astype(F32))
        for k, tile in enumerate(join_pieces(pieces)):
            coeffs[:, 128 * k : 128 * k + 128] = tile * factor_ref[0:1, 128 * k : 128 * k + 128]
        for j in range(OWNERS):
            force_rows[32 * j : 32 * j + 32, :] = forcing_ref[j].astype(F32)

    for r in range(6):
        h, f = r // 3, r % 3
        real = coeffs[pl.ds(lat * 12 + h * 6 + f, 1), :]
        imag = coeffs[pl.ds(lat * 12 + h * 6 + 3 + f, 1), :]
        oc, os = outer_ref[lat, 0], outer_ref[lat, 1]
        turned[32 * r : 32 * r + 32, 0:WAVES] = (real * oc - imag * os).astype(BF16)
        turned[32 * r : 32 * r + 32, WAVES:] = (-(real * os + imag * oc)).astype(BF16)
    rows = lax.dot_general(turned[...], inner_ref[lat], NT, preferred_element_type=F32)
    inside = inside_mask(me, lat)
    for r in range(6):
        value = jnp.where(inside, rows[32 * r : 32 * r + 32, :], 0.0).astype(BF16).astype(F32)
        values[32 * r : 32 * r + 32, :] = value
        grid_rows[pl.ds(r, OWNERS, stride=8), :] = value[:, 0:128]
    for h in range(2):
        tails = [
            jnp.concatenate(
                [values[32 * r : 32 * r + 32, 128:BROWS], jnp.zeros((OWNERS, 256 - BROWS), F32)], axis=1
            )
            for r in range(3 * h, 3 * h + 3)
        ]
        grid_rows[pl.ds(6 + h, OWNERS, stride=8), :] = join_tails(*tails)
    send_ref[...] = grid_rows[...].reshape(OWNERS, 8, 128).astype(BF16)
    for r in range(6):
        h, f = r // 3, r % 3
        other = h * 3 + (f + 1) % 3
        product = values[32 * r : 32 * r + 32, :] * values[32 * other : 32 * other + 32, :]
        tail = tail_of(force_rows[pl.ds(lat * 8 + 6 + h, OWNERS, stride=32), :], f)
        force = jnp.concatenate(
            [force_rows[pl.ds(lat * 8 + r, OWNERS, stride=32), :], tail[:, 0 : BROWS - 128]], axis=1
        )
        samples[32 * r : 32 * r + 32, :] = jnp.where(inside, product + force, 0.0).astype(BF16)
    length = jnp.full((1, 256), (5012 + 16 * me + 4 * lat).astype(F32), F32)
    scale = weight_ref[me * 4 + lat] * lax.rsqrt(length)
    data = samples[...]
    for n in range(0, WAVES, 256):
        part_c = lax.dot_general(data, inner_ref[lat, :, n : n + 256], NN, preferred_element_type=F32)
        part_s = lax.dot_general(
            data, inner_ref[lat, :, WAVES + n : WAVES + n + 256], NN, preferred_element_type=F32
        )
        oc, os = outer_ref[lat, 0, :, n : n + 256], outer_ref[lat, 1, :, n : n + 256]
        for r in range(6):
            h, f = r // 3, r % 3
            pc, ps = part_c[32 * r : 32 * r + 32, :], part_s[32 * r : 32 * r + 32, :]
            real = jnp.sum(pc * oc - ps * os, axis=0, keepdims=True)
            imag = jnp.sum(ps * oc + pc * os, axis=0, keepdims=True)
            sums[pl.ds(lat * 12 + h * 6 + f, 1), n : n + 256] = real * scale
            sums[pl.ds(lat * 12 + h * 6 + 3 + f, 1), n : n + 256] = -imag * scale

    @pl.when(lat == 3)
    def _():
        for d, ref in enumerate((own_ref, other_ref)):
            for s in range(4):
                for w in range(2):
                    piece = cut_piece(sums, (d * 4 + s) * 2 + w)
                    ref[s, :, 128 * w : 128 * w + 128] = piece.astype(BF16)
        fetch.wait()


def transform_rows(me, weight, kept, got, forcing, outer, inner, factor, legendre):
    slots = legendre.shape[2]
    return pl.pallas_call(
        row_kernel,
        grid_spec=pltpu.PrefetchScalarGridSpec(
            num_scalar_prefetch=2,
            grid=(4,),
            in_specs=[
                pl.BlockSpec((4, 48, 256), lambda i, *_: (0, 0, 0)),
                pl.BlockSpec((4, 48, 256), lambda i, *_: (0, 0, 0)),
                pl.BlockSpec(memory_space=pltpu.VMEM),
                pl.BlockSpec(memory_space=pltpu.VMEM),
                pl.BlockSpec(memory_space=pltpu.VMEM),
                pl.BlockSpec(memory_space=pltpu.VMEM),
                pl.BlockSpec(memory_space=pltpu.HBM),
            ],
            out_specs=[
                pl.BlockSpec((OWNERS, 8, 128), lambda i, *_: (0, i, 0)),
                pl.BlockSpec((4, 48, 256), lambda i, *_: (0, 0, 0)),
                pl.BlockSpec((4, 48, 256), lambda i, *_: (0, 0, 0)),
                pl.BlockSpec(memory_space=pltpu.VMEM),
            ],
            scratch_shapes=[
                pltpu.SemaphoreType.DMA,
                pltpu.VMEM((48, WAVES), F32),
                pltpu.VMEM((192, 2 * WAVES), BF16),
                pltpu.VMEM((OWNERS * 8, 128), F32),
                pltpu.VMEM((1024, 128), F32),
                pltpu.VMEM((192, BROWS), F32),
                pltpu.VMEM((192, BROWS), BF16),
                pltpu.VMEM((48, WAVES), F32),
            ],
        ),
        out_shape=[
            pltpu.HBM((OWNERS, 32, 128), BF16),
            jax.ShapeDtypeStruct((4, 48, 256), BF16),
            jax.ShapeDtypeStruct((4, 48, 256), BF16),
            pltpu.VMEM((PAIR_BLOCK, 32, slots), BF16),
        ],
        compiler_params=vmem_params(14),
        cost_estimate=pl.CostEstimate(flops=1_400_000_000, bytes_accessed=6_000_000, transcendentals=0),
        name="transform_rows",
    )(
        me,
        weight,
        kept,
        got,
        forcing,
        outer,
        inner,
        factor,
        legendre,
    )


def legendre_direct_kernel(
    pw_ref, me_ref, first_ref, second_ref, third_ref, fourth_ref, leg_ref, block_ref, out_ref, held, arrived, by_lat, by_pair
):
    step = pl.program_id(0)
    slots = leg_ref.shape[2]

    @pl.when(step == 0)
    def _():
        legendre_start(leg_ref, held, arrived, 1)
        x, core = me_ref[0] // 2, me_ref[0] % 2
        for s, ref in enumerate((first_ref, second_ref, third_ref, fourth_ref)):
            for d in range(2):
                source = ((x + s) % 4) * 2 + (core + d) % 2
                rows = pl.ds(pl.multiple_of(source * 48, 8), 48)
                for w in range(2):
                    by_lat[w, rows, :] = ref[d, :, 128 * w : 128 * w + 128].astype(F32)
        for w in range(2):
            for c in range(6):
                north = by_lat[w, pl.ds(c, 32, stride=12), :]
                south = by_lat[w, pl.ds(6 + c, 32, stride=12), :]
                for odd, value in enumerate((north + south, north - south)):
                    turned = jnp.concatenate([value, jnp.zeros((96, 128), F32)], axis=0).T
                    row = (w * 2 + odd) * 8 + (c % 3) * 2 + c // 3
                    by_pair[pl.ds(row, PAIRS, stride=32), :] = turned[0:PAIRS, :]

    slot = lax.broadcasted_iota(jnp.int32, (8, slots), 1)
    even = slot % 2 == 0
    valid = slot <= TRUNCATION + 1

    def sum_block(table):
        for k in range(PAIR_BLOCK):
            pair = step * PAIR_BLOCK + k
            wave = pw_ref[me_ref[0] * PAIRS + pair]
            lhs = by_pair[pl.ds(pl.multiple_of(pair * 32, 32), 32), :][:, 0:32].astype(BF16)
            sums = lax.dot_general(lhs, table(k), NN, preferred_element_type=F32)
            first = jnp.where(even, sums[0:8], sums[8:16])
            second = jnp.where((slot + wave) % 2 == 0, sums[16:24], sums[24:32])
            value = jnp.where(slot <= TRUNCATION - wave, first, second)
            value = jnp.where(valid, value, 0.0).astype(BF16)
            for f in range(FIELDS):
                out_ref[k, f] = value[2 * f : 2 * f + 2]

    @pl.when(step == 0)
    def _():
        sum_block(lambda k: block_ref[k])

    @pl.when(step > 0)
    def _():
        legendre_block(leg_ref, held, arrived, step).wait()
        sum_block(lambda k: held[step * PAIR_BLOCK + k])


def legendre_direct(pair_wave, me, came, legendre, block):
    slots = legendre.shape[2]
    return pl.pallas_call(
        legendre_direct_kernel,
        grid_spec=pltpu.PrefetchScalarGridSpec(
            num_scalar_prefetch=2,
            grid=(PAIRS // PAIR_BLOCK,),
            in_specs=[pl.BlockSpec((2, 48, 256), lambda i, *_: (0, 0, 0))] * 4
            + [pl.BlockSpec(memory_space=pltpu.HBM), pl.BlockSpec(memory_space=pltpu.VMEM)],
            out_specs=pl.BlockSpec((PAIR_BLOCK, FIELDS, 2, slots), lambda i, *_: (i, 0, 0, 0)),
            scratch_shapes=[
                pltpu.VMEM((PAIRS, 32, slots), BF16),
                pltpu.SemaphoreType.DMA((PAIRS // PAIR_BLOCK,)),
                pltpu.VMEM((2, 384, 128), F32),
                pltpu.VMEM((32 * PAIRS, 128), F32),
            ],
        ),
        out_shape=jax.ShapeDtypeStruct((PAIRS, FIELDS, 2, slots), BF16),
        compiler_params=vmem_params(16),
        cost_estimate=pl.CostEstimate(flops=2 * 80 * 32 * 32 * 1288, bytes_accessed=9_000_000, transcendentals=0),
        name="legendre_direct",
    )(pair_wave, me, *came, legendre, block)


def to_chip(value, distance):
    return lax.ppermute(value, "aa", [(i, ((i // 2 + distance) % 4) * 2 + i % 2) for i in range(8)])


def to_other_core(value):
    return lax.ppermute(value, "aa", [(i, i ^ 1) for i in range(8)])


def per_device(spec_in, legendre, pair_wave, quad_weight, forcing):
    me = lax.axis_index("aa").astype(jnp.int32).reshape(1)
    legendre = pltpu.with_memory_space_constraint(legendre, pltpu.HBM)
    wave_table = pltpu.with_memory_space_constraint(pair_wave, pltpu.HBM)
    spec = jnp.swapaxes(spec_in.reshape(PAIRS, 2, FIELDS, -1), 1, 2)
    spec = pltpu.with_memory_space_constraint(spec, pltpu.HBM)
    forcing_send, spec = pack_rows(forcing.reshape(24, OWNERS, COLS), spec)
    forcing_here = lax.all_to_all(forcing_send, "ba", split_axis=0, concat_axis=0, tiled=True)
    fourier = legendre_inverse(wave_table, me, legendre, spec)
    pairs = pair_wave.astype(F32).reshape(8, PAIRS)
    waves = jnp.pad(jnp.stack([pairs, TRUNCATION - pairs], axis=1), ((0, 0), (0, 0), (0, 48)))
    waves, forcing_here = lax.optimization_barrier((waves, forcing_here))
    outer, inner, factor = phase_tables(me, waves)
    came = [fourier[0]] + [to_chip(fourier[s], s) for s in range(1, 4)]
    *came, factor = lax.optimization_barrier((*came, factor))
    kept = jnp.stack([c[0] for c in came])
    got = to_other_core(jnp.stack([c[1] for c in came]))
    grid_send, own, other, block = transform_rows(
        me, quad_weight, kept, got, forcing_here, outer, inner, factor, legendre
    )
    staying, grid_send = lax.optimization_barrier((own[0], grid_send))
    grid_came = lax.all_to_all(grid_send, "ba", split_axis=0, concat_axis=0, tiled=True)
    passed = to_other_core(other)
    parts = [jnp.stack([own[s] if s else staying, passed[s]]) for s in range(4)]
    came = [parts[0]] + [to_chip(parts[s], -s) for s in range(1, 4)]
    spec_out = legendre_direct(wave_table, me, came, legendre, block)
    grid = unpack_rows(grid_came)
    return (
        grid.reshape(8, FIELDS, OWNERS, COLS),
        jnp.swapaxes(spec_out, 1, 2).reshape(PAIRS, 2, FIELDS, 1, -1),
    )


def solution(mesh):
    placed = (
        P("aa", None, None, "ba", None),
        P("aa", None, None),
        P(),
        P(),
        P("aa", None, None, "ba"),
    )
    return jax.shard_map(
        per_device,
        mesh=mesh,
        in_specs=placed,
        out_specs=(P("aa", None, None, "ba"), P("aa", None, None, "ba", None)),
        check_vma=False,
    )
```

```python
import functools
import math

import jax
import jax.numpy as jnp
from jax import lax
from jax.experimental import pallas as pl
from jax.experimental.pallas import tpu as pltpu
from jax.sharding import PartitionSpec as P

TRUNCATION = 1279
FIELDS = 3
PAIRS = 80
WAVES = 1280
COLS = 164
OWNERS = 32
BROWS = 176
TAIL = COLS - 128
PAIR_BLOCK = 20
F32 = jnp.float32
BF16 = jnp.bfloat16
NT = (((1,), (1,)), ((), ()))
NN = (((1,), (0,)), ((), ()))


def vmem_params(mib):
    return pltpu.CompilerParams(vmem_limit_bytes=mib << 20)


def join_tails(first, second, third):
    return first + pltpu.roll(second, TAIL, axis=1) + pltpu.roll(third, 2 * TAIL, axis=1)


def tail_of(joined, field):
    return pltpu.roll(joined, 128 - TAIL * field, axis=1) if field else joined


def pack_kernel(x_ref, spec_ref, o_ref, spec_out, held, arrived, rows, fetched):
    fetch = pltpu.make_async_copy(spec_ref, spec_out, fetched)

    def part(k):
        return pltpu.make_async_copy(x_ref.at[pl.ds(6 * k, 6)], held.at[pl.ds(6 * k, 6)], arrived.at[k])

    for k in range(4):
        part(k).start()
    fetch.start()
    for k in range(4):
        part(k).wait()
        for pair in (2 * k, 2 * k + 1):
            tails = []
            for f in range(FIELDS):
                x = held[3 * pair + f].astype(F32)
                rows[k, pl.ds(pair % 2 * 3 + f, OWNERS, stride=8), :] = x[:, 0:128]
                tails.append(jnp.concatenate([x[:, 128:COLS], jnp.zeros((OWNERS, 128 - TAIL), F32)], axis=1))
            rows[k, pl.ds(6 + pair % 2, OWNERS, stride=8), :] = join_tails(*tails)
        o_ref[:, 8 * k : 8 * k + 8, :] = rows[k].reshape(OWNERS, 8, 128).astype(BF16)
    fetch.wait()


def pack_rows(x, spec):
    slots = spec.shape[3]
    return pl.pallas_call(
        pack_kernel,
        in_specs=[pl.BlockSpec(memory_space=pltpu.HBM)] * 2,
        out_specs=[pl.BlockSpec(memory_space=pltpu.VMEM)] * 2,
        out_shape=[
            jax.ShapeDtypeStruct((OWNERS, 32, 128), BF16),
            pltpu.VMEM((PAIRS, FIELDS, 2, slots), BF16),
        ],
        scratch_shapes=[
            pltpu.VMEM((24, OWNERS, COLS), BF16),
            pltpu.SemaphoreType.DMA((4,)),
            pltpu.VMEM((4, OWNERS * 8, 128), F32),
            pltpu.SemaphoreType.DMA,
        ],
        compiler_params=vmem_params(4),
        cost_estimate=pl.CostEstimate(flops=0, bytes_accessed=800_000, transcendentals=0),
        name="pack_rows",
    )(pltpu.with_memory_space_constraint(x, pltpu.HBM), spec)


def unpack_kernel(x_ref, o_ref, rows, held, written):
    copies = []
    for lat in range(4):
        rows[lat] = x_ref[:, 8 * lat : 8 * lat + 8, :].astype(F32).reshape(OWNERS * 8, 128)
        for h in range(2):
            joined = rows[lat, pl.ds(6 + h, OWNERS, stride=8), :]
            for f in range(FIELDS):
                own = rows[lat, pl.ds(3 * h + f, OWNERS, stride=8), :]
                held[6 * lat + 3 * h + f, :, 0:128] = own.astype(BF16)
                held[6 * lat + 3 * h + f, :, 128:COLS] = tail_of(joined, f)[:, 0:TAIL].astype(BF16)
        part = pl.ds(6 * lat, 6)
        copies.append(pltpu.make_async_copy(held.at[part], o_ref.at[part], written.at[lat]))
        copies[lat].start()
    for copy in copies:
        copy.wait()


def unpack_rows(x):
    return pl.pallas_call(
        unpack_kernel,
        in_specs=[pl.BlockSpec(memory_space=pltpu.VMEM)],
        out_specs=pl.BlockSpec(memory_space=pltpu.HBM),
        out_shape=pltpu.HBM((24, OWNERS, COLS), BF16),
        scratch_shapes=[
            pltpu.VMEM((4, OWNERS * 8, 128), F32),
            pltpu.VMEM((24, OWNERS, COLS), BF16),
            pltpu.SemaphoreType.DMA((4,)),
        ],
        compiler_params=vmem_params(4),
        cost_estimate=pl.CostEstimate(flops=0, bytes_accessed=800_000, transcendentals=0),
        name="unpack_rows",
    )(x)


def legendre_block(leg_ref, held, arrived, k):
    rows = pl.ds(pl.multiple_of(k * PAIR_BLOCK, PAIR_BLOCK), PAIR_BLOCK)
    return pltpu.make_async_copy(leg_ref.at[rows], held.at[rows], arrived.at[k])


def legendre_start(leg_ref, held, arrived, first):
    for k in range(first, PAIRS // PAIR_BLOCK):
        legendre_block(leg_ref, held, arrived, k).start()


def legendre_inverse_kernel(
    pw_ref, me_ref, leg_ref, spec_ref, out_ref, held, arrived, by_pair, by_lat
):
    step = pl.program_id(0)
    slots = leg_ref.shape[2]
    slot = lax.broadcasted_iota(jnp.int32, (8, slots), 1)
    alternate = jnp.where(slot % 2 == 0, 1.0, -1.0).astype(F32)
    valid = slot <= TRUNCATION + 1
    row = lax.broadcasted_iota(jnp.int32, (32, 32), 0)

    def sum_block(table):
        for k in range(PAIR_BLOCK):
            pair = step * PAIR_BLOCK + k
            wave = pw_ref[me_ref[0] * PAIRS + pair]
            first = slot <= TRUNCATION - wave
            a = jnp.concatenate(
                [spec_ref[pair, f].astype(F32) for f in range(FIELDS)] + [jnp.zeros((2, slots), F32)], axis=0
            )
            a = jnp.where(valid, a, 0.0)
            b = a * alternate
            lhs = jnp.concatenate(
                [
                    jnp.where(first, a, 0.0),
                    jnp.where(first, b, 0.0),
                    jnp.where(first, 0.0, a),
                    jnp.where(first, 0.0, b),
                ],
                axis=0,
            ).astype(BF16)
            sums = lax.dot_general(lhs, table(k), NT, preferred_element_type=F32)
            sign = (1 - 2 * (wave % 2)).astype(F32)
            sums = jnp.where(row >= 24, sums * sign, sums)
            by_pair[pl.ds(pair, 32, stride=PAIRS), :] = jnp.concatenate(
                [sums, jnp.zeros((32, 96), F32)], axis=1
            )

    @pl.when(step == 0)
    def _():
        legendre_start(leg_ref, held, arrived, 0)

    legendre_block(leg_ref, held, arrived, step).wait()
    sum_block(lambda k: held[step * PAIR_BLOCK + k])

    @pl.when(step == pl.num_programs(0) - 1)
    def _():
        for half in range(4):
            h, w = half % 2, half // 2
            for c in range(6):
                start = (half * 8 + c) * PAIRS
                turned = jnp.concatenate(
                    [by_pair[start : start + PAIRS, :], jnp.zeros((48, 128), F32)], axis=0
                ).T
                by_lat[w, pl.ds(h * 6 + (c % 2) * 3 + c // 2, 32, stride=12), :] = turned[0:32, :]
        x, core = me_ref[0] // 2, me_ref[0] % 2
        for s in range(4):
            for d in range(2):
                dest = ((x + s) % 4) * 2 + (core + d) % 2
                rows = pl.ds(pl.multiple_of(dest * 48, 8), 48)
                out_ref[s, d, :, 0:128] = by_lat[0, rows, :].astype(BF16)
                out_ref[s, d, :, 128:256] = by_lat[1, rows, :].astype(BF16)


def legendre_inverse(pair_wave, me, legendre, spec):
    slots = legendre.shape[2]
    return pl.pallas_call(
        legendre_inverse_kernel,
        grid_spec=pltpu.PrefetchScalarGridSpec(
            num_scalar_prefetch=2,
            grid=(PAIRS // PAIR_BLOCK,),
            in_specs=[
                pl.BlockSpec(memory_space=pltpu.HBM),
                pl.BlockSpec(memory_space=pltpu.VMEM),
            ],
            out_specs=pl.BlockSpec((4, 2, 48, 256), lambda i, *_: (0, 0, 0, 0)),
            scratch_shapes=[
                pltpu.VMEM((PAIRS, 32, slots), BF16),
                pltpu.SemaphoreType.DMA((PAIRS // PAIR_BLOCK,)),
                pltpu.VMEM((32 * PAIRS, 128), F32),
                pltpu.VMEM((2, 384, 128), F32),
            ],
        ),
        out_shape=jax.ShapeDtypeStruct((4, 2, 48, 256), BF16),
        compiler_params=vmem_params(16),
        cost_estimate=pl.CostEstimate(flops=2 * 80 * 32 * 32 * 1288, bytes_accessed=9_000_000, transcendentals=0),
        name="legendre_inverse",
    )(pair_wave, me, legendre, spec)


def join_pieces(pieces):
    lane = lax.broadcasted_iota(jnp.int32, pieces[0].shape, 1)
    rolled = [pltpu.roll(p, (80 * i) % 128, axis=1) if (80 * i) % 128 else p for i, p in enumerate(pieces)]
    tiles = []
    for k in range(10):
        tile = None
        for i in range(16):
            low, high = 80 * i - 128 * k, 80 * i + 80 - 128 * k
            if high <= 0 or low >= 128:
                continue
            tile = rolled[i] if tile is None else jnp.where(lane >= low, rolled[i], tile)
        tiles.append(tile)
    return tiles


def cut_piece(ref, i):
    tile, shift = (80 * i) // 128, (80 * i) % 128
    low = ref[:, tile * 128 : tile * 128 + 128]
    if shift == 0:
        return low
    low = pltpu.roll(low, 128 - shift, axis=1)
    if shift + 80 <= 128:
        return low
    high = pltpu.roll(ref[:, tile * 128 + 128 : tile * 128 + 256], 128 - shift, axis=1)
    lane = lax.broadcasted_iota(jnp.int32, low.shape, 1)
    return jnp.where(lane < 128 - shift, low, high)


def cos_sin(turn, length):
    times = jnp.floor(turn * (1.0 / length) + 0.5)
    u = (turn - times * length) * (math.pi / length)
    u2 = u * u
    s = u * (
        1.0
        + u2
        * (
            -1.0 / 6
            + u2 * (1.0 / 120 + u2 * (-1.0 / 5040 + u2 * (1.0 / 362880 + u2 * (-1.0 / 39916800))))
        )
    )
    c = 1.0 + u2 * (
        -0.5
        + u2
        * (
            1.0 / 24
            + u2
            * (-1.0 / 720 + u2 * (1.0 / 40320 + u2 * (-1.0 / 3628800 + u2 * (1.0 / 479001600))))
        )
    )
    return 1.0 - 2.0 * s * s, 2.0 * s * c


def table_kernel(me_ref, waves_ref, outer_ref, inner_ref, factor_ref, wave_row):
    lat = pl.program_id(0)
    me = me_ref[0]
    x, core = me // 2, me % 2

    @pl.when(lat == 0)
    def _():
        pieces = []
        for d in range(2):
            for s in range(4):
                source = ((x + 4 - s) % 4) * 2 + (core + d) % 2
                for w in range(2):
                    pieces.append(jnp.broadcast_to(waves_ref[source, w : w + 1, :], (8, 128)))
        for k, tile in enumerate(join_pieces(pieces)):
            wave_row[:, 128 * k : 128 * k + 128] = tile
            factor_ref[:, 128 * k : 128 * k + 128] = jnp.where(tile == 0.0, 1.0, 2.0)

    length = jnp.full((1, 1), (5012 + 16 * me + 4 * lat).astype(F32), F32)
    wave = wave_row[...]
    eight = lax.broadcasted_iota(jnp.int32, (8, WAVES), 0).astype(F32)
    low_c, low_s = cos_sin(wave * (eight * COLS), length)
    single = lax.broadcasted_iota(jnp.int32, (8, WAVES), 0)
    steps = jnp.where(single < 4, single * (8 * COLS), (single - 4) * 64).astype(F32)
    step_c, step_s = cos_sin(wave * steps, length)
    high_c, high_s = step_c, step_s
    for k in range(4):
        hc, hs = high_c[k : k + 1, :], high_s[k : k + 1, :]
        outer_ref[0, 0, 8 * k : 8 * k + 8, :] = low_c * hc - low_s * hs
        outer_ref[0, 1, 8 * k : 8 * k + 8, :] = low_s * hc + low_c * hs
    low_c, low_s = cos_sin(wave * eight, length)
    first_c, first_s = cos_sin(wave * (eight * 8.0), length)
    for block in range(3):
        high_c, high_s = first_c, first_s
        if block:
            sc, ss = step_c[4 + block : 5 + block, :], step_s[4 + block : 5 + block, :]
            high_c, high_s = first_c * sc - first_s * ss, first_s * sc + first_c * ss
        for k in range(0, 8, 2):
            base = 64 * block + 8 * k
            if base >= BROWS:
                continue
            parts_c, parts_s = [], []
            for kk in (k, k + 1):
                hc, hs = high_c[kk : kk + 1, :], high_s[kk : kk + 1, :]
                parts_c.append(low_c * hc - low_s * hs)
                parts_s.append(low_s * hc + low_c * hs)
            inner_ref[0, base : base + 16, 0:WAVES] = jnp.concatenate(parts_c, axis=0).astype(BF16)
            inner_ref[0, base : base + 16, WAVES:] = jnp.concatenate(parts_s, axis=0).astype(BF16)


def phase_tables(me, waves):
    return pl.pallas_call(
        table_kernel,
        grid_spec=pltpu.PrefetchScalarGridSpec(
            num_scalar_prefetch=1,
            grid=(4,),
            in_specs=[pl.BlockSpec((8, 2, 128), lambda i, *_: (0, 0, 0))],
            out_specs=[
                pl.BlockSpec((1, 2, OWNERS, WAVES), lambda i, *_: (i, 0, 0, 0)),
                pl.BlockSpec((1, BROWS, 2 * WAVES), lambda i, *_: (i, 0, 0)),
                pl.BlockSpec((8, WAVES), lambda i, *_: (0, 0)),
            ],
            scratch_shapes=[pltpu.VMEM((8, WAVES), F32)],
        ),
        out_shape=[
            jax.ShapeDtypeStruct((4, 2, OWNERS, WAVES), F32),
            jax.ShapeDtypeStruct((4, BROWS, 2 * WAVES), BF16),
            jax.ShapeDtypeStruct((8, WAVES), F32),
        ],
        compiler_params=vmem_params(8),
        cost_estimate=pl.CostEstimate(flops=40_000_000, bytes_accessed=5_000_000, transcendentals=0),
        name="phase_tables",
    )(me, waves)


def inside_mask(me, lat):
    length = 5012 + 16 * me + 4 * lat
    owner = lax.broadcasted_iota(jnp.int32, (OWNERS, BROWS), 0)
    col = lax.broadcasted_iota(jnp.int32, (OWNERS, BROWS), 1)
    return (col < COLS) & (owner * COLS + col < length)


def row_kernel(
    me_ref,
    weight_ref,
    kept_ref,
    got_ref,
    forcing_ref,
    outer_ref,
    inner_ref,
    factor_ref,
    leg_ref,
    send_ref,
    own_ref,
    other_ref,
    block_ref,
    fetched,
    coeffs,
    turned,
    grid_rows,
    force_rows,
    values,
    samples,
    sums,
):
    lat = pl.program_id(0)
    me = me_ref[0]

    fetch = pltpu.make_async_copy(leg_ref.at[pl.ds(0, PAIR_BLOCK)], block_ref, fetched)

    @pl.when(lat == 0)
    def _():
        fetch.start()
        pieces = []
        for ref in (kept_ref, got_ref):
            for s in range(4):
                for w in range(2):
                    pieces.append(ref[s, :, 128 * w : 128 * w + 128].astype(F32))
        for k, tile in enumerate(join_pieces(pieces)):
            coeffs[:, 128 * k : 128 * k + 128] = tile * factor_ref[0:1, 128 * k : 128 * k + 128]
        for j in range(OWNERS):
            force_rows[32 * j : 32 * j + 32, :] = forcing_ref[j].astype(F32)

    for r in range(6):
        h, f = r // 3, r % 3
        real = coeffs[pl.ds(lat * 12 + h * 6 + f, 1), :]
        imag = coeffs[pl.ds(lat * 12 + h * 6 + 3 + f, 1), :]
        oc, os = outer_ref[lat, 0], outer_ref[lat, 1]
        turned[32 * r : 32 * r + 32, 0:WAVES] = (real * oc - imag * os).astype(BF16)
        turned[32 * r : 32 * r + 32, WAVES:] = (-(real * os + imag * oc)).astype(BF16)
    rows = lax.dot_general(turned[...], inner_ref[lat], NT, preferred_element_type=F32)
    inside = inside_mask(me, lat)
    for r in range(6):
        value = jnp.where(inside, rows[32 * r : 32 * r + 32, :], 0.0).astype(BF16).astype(F32)
        values[32 * r : 32 * r + 32, :] = value
        grid_rows[pl.ds(r, OWNERS, stride=8), :] = value[:, 0:128]
    for h in range(2):
        tails = [
            jnp.concatenate(
                [values[32 * r : 32 * r + 32, 128:BROWS], jnp.zeros((OWNERS, 256 - BROWS), F32)], axis=1
            )
            for r in range(3 * h, 3 * h + 3)
        ]
        grid_rows[pl.ds(6 + h, OWNERS, stride=8), :] = join_tails(*tails)
    send_ref[...] = grid_rows[...].reshape(OWNERS, 8, 128).astype(BF16)
    for r in range(6):
        h, f = r // 3, r % 3
        other = h * 3 + (f + 1) % 3
        product = values[32 * r : 32 * r + 32, :] * values[32 * other : 32 * other + 32, :]
        tail = tail_of(force_rows[pl.ds(lat * 8 + 6 + h, OWNERS, stride=32), :], f)
        force = jnp.concatenate(
            [force_rows[pl.ds(lat * 8 + r, OWNERS, stride=32), :], tail[:, 0 : BROWS - 128]], axis=1
        )
        samples[32 * r : 32 * r + 32, :] = jnp.where(inside, product + force, 0.0).astype(BF16)
    length = jnp.full((1, 256), (5012 + 16 * me + 4 * lat).astype(F32), F32)
    scale = weight_ref[me * 4 + lat] * lax.rsqrt(length)
    data = samples[...]
    for n in range(0, WAVES, 256):
        part_c = lax.dot_general(data, inner_ref[lat, :, n : n + 256], NN, preferred_element_type=F32)
        part_s = lax.dot_general(
            data, inner_ref[lat, :, WAVES + n : WAVES + n + 256], NN, preferred_element_type=F32
        )
        oc, os = outer_ref[lat, 0, :, n : n + 256], outer_ref[lat, 1, :, n : n + 256]
        for r in range(6):
            h, f = r // 3, r % 3
            pc, ps = part_c[32 * r : 32 * r + 32, :], part_s[32 * r : 32 * r + 32, :]
            real = jnp.sum(pc * oc - ps * os, axis=0, keepdims=True)
            imag = jnp.sum(ps * oc + pc * os, axis=0, keepdims=True)
            sums[pl.ds(lat * 12 + h * 6 + f, 1), n : n + 256] = real * scale
            sums[pl.ds(lat * 12 + h * 6 + 3 + f, 1), n : n + 256] = -imag * scale

    @pl.when(lat == 3)
    def _():
        for d, ref in enumerate((own_ref, other_ref)):
            for s in range(4):
                for w in range(2):
                    piece = cut_piece(sums, (d * 4 + s) * 2 + w)
                    ref[s, :, 128 * w : 128 * w + 128] = piece.astype(BF16)
        fetch.wait()


def transform_rows(me, weight, kept, got, forcing, outer, inner, factor, legendre):
    slots = legendre.shape[2]
    return pl.pallas_call(
        row_kernel,
        grid_spec=pltpu.PrefetchScalarGridSpec(
            num_scalar_prefetch=2,
            grid=(4,),
            in_specs=[
                pl.BlockSpec((4, 48, 256), lambda i, *_: (0, 0, 0)),
                pl.BlockSpec((4, 48, 256), lambda i, *_: (0, 0, 0)),
                pl.BlockSpec(memory_space=pltpu.VMEM),
                pl.BlockSpec(memory_space=pltpu.VMEM),
                pl.BlockSpec(memory_space=pltpu.VMEM),
                pl.BlockSpec(memory_space=pltpu.VMEM),
                pl.BlockSpec(memory_space=pltpu.HBM),
            ],
            out_specs=[
                pl.BlockSpec((OWNERS, 8, 128), lambda i, *_: (0, i, 0)),
                pl.BlockSpec((4, 48, 256), lambda i, *_: (0, 0, 0)),
                pl.BlockSpec((4, 48, 256), lambda i, *_: (0, 0, 0)),
                pl.BlockSpec(memory_space=pltpu.VMEM),
            ],
            scratch_shapes=[
                pltpu.SemaphoreType.DMA,
                pltpu.VMEM((48, WAVES), F32),
                pltpu.VMEM((192, 2 * WAVES), BF16),
                pltpu.VMEM((OWNERS * 8, 128), F32),
                pltpu.VMEM((1024, 128), F32),
                pltpu.VMEM((192, BROWS), F32),
                pltpu.VMEM((192, BROWS), BF16),
                pltpu.VMEM((48, WAVES), F32),
            ],
        ),
        out_shape=[
            pltpu.HBM((OWNERS, 32, 128), BF16),
            jax.ShapeDtypeStruct((4, 48, 256), BF16),
            jax.ShapeDtypeStruct((4, 48, 256), BF16),
            pltpu.VMEM((PAIR_BLOCK, 32, slots), BF16),
        ],
        compiler_params=vmem_params(14),
        cost_estimate=pl.CostEstimate(flops=1_400_000_000, bytes_accessed=6_000_000, transcendentals=0),
        name="transform_rows",
    )(
        me,
        weight,
        kept,
        got,
        forcing,
        outer,
        inner,
        factor,
        legendre,
    )


def legendre_direct_kernel(
    pw_ref, me_ref, first_ref, second_ref, third_ref, fourth_ref, leg_ref, block_ref, out_ref, held, arrived, by_lat, by_pair
):
    step = pl.program_id(0)
    slots = leg_ref.shape[2]

    @pl.when(step == 0)
    def _():
        legendre_start(leg_ref, held, arrived, 1)
        x, core = me_ref[0] // 2, me_ref[0] % 2
        for s, ref in enumerate((first_ref, second_ref, third_ref, fourth_ref)):
            for d in range(2):
                source = ((x + s) % 4) * 2 + (core + d) % 2
                rows = pl.ds(pl.multiple_of(source * 48, 8), 48)
                for w in range(2):
                    by_lat[w, rows, :] = ref[d, :, 128 * w : 128 * w + 128].astype(F32)
        for w in range(2):
            for c in range(6):
                north = by_lat[w, pl.ds(c, 32, stride=12), :]
                south = by_lat[w, pl.ds(6 + c, 32, stride=12), :]
                for odd, value in enumerate((north + south, north - south)):
                    turned = jnp.concatenate([value, jnp.zeros((96, 128), F32)], axis=0).T
                    row = (w * 2 + odd) * 8 + (c % 3) * 2 + c // 3
                    by_pair[pl.ds(row, PAIRS, stride=32), :] = turned[0:PAIRS, :]

    slot = lax.broadcasted_iota(jnp.int32, (8, slots), 1)
    even = slot % 2 == 0
    valid = slot <= TRUNCATION + 1

    def sum_block(table):
        for k in range(PAIR_BLOCK):
            pair = step * PAIR_BLOCK + k
            wave = pw_ref[me_ref[0] * PAIRS + pair]
            lhs = by_pair[pl.ds(pl.multiple_of(pair * 32, 32), 32), :][:, 0:32].astype(BF16)
            sums = lax.dot_general(lhs, table(k), NN, preferred_element_type=F32)
            first = jnp.where(even, sums[0:8], sums[8:16])
            second = jnp.where((slot + wave) % 2 == 0, sums[16:24], sums[24:32])
            value = jnp.where(slot <= TRUNCATION - wave, first, second)
            value = jnp.where(valid, value, 0.0).astype(BF16)
            for f in range(FIELDS):
                out_ref[k, f] = value[2 * f : 2 * f + 2]

    @pl.when(step == 0)
    def _():
        sum_block(lambda k: block_ref[k])

    @pl.when(step > 0)
    def _():
        legendre_block(leg_ref, held, arrived, step).wait()
        sum_block(lambda k: held[step * PAIR_BLOCK + k])


def legendre_direct(pair_wave, me, came, legendre, block):
    slots = legendre.shape[2]
    return pl.pallas_call(
        legendre_direct_kernel,
        grid_spec=pltpu.PrefetchScalarGridSpec(
            num_scalar_prefetch=2,
            grid=(PAIRS // PAIR_BLOCK,),
            in_specs=[pl.BlockSpec((2, 48, 256), lambda i, *_: (0, 0, 0))] * 4
            + [pl.BlockSpec(memory_space=pltpu.HBM), pl.BlockSpec(memory_space=pltpu.VMEM)],
            out_specs=pl.BlockSpec((PAIR_BLOCK, FIELDS, 2, slots), lambda i, *_: (i, 0, 0, 0)),
            scratch_shapes=[
                pltpu.VMEM((PAIRS, 32, slots), BF16),
                pltpu.SemaphoreType.DMA((PAIRS // PAIR_BLOCK,)),
                pltpu.VMEM((2, 384, 128), F32),
                pltpu.VMEM((32 * PAIRS, 128), F32),
            ],
        ),
        out_shape=jax.ShapeDtypeStruct((PAIRS, FIELDS, 2, slots), BF16),
        compiler_params=vmem_params(16),
        cost_estimate=pl.CostEstimate(flops=2 * 80 * 32 * 32 * 1288, bytes_accessed=9_000_000, transcendentals=0),
        name="legendre_direct",
    )(pair_wave, me, *came, legendre, block)


def to_chip(value, distance):
    return lax.ppermute(value, "aa", [(i, ((i // 2 + distance) % 4) * 2 + i % 2) for i in range(8)])


def to_other_core(value):
    return lax.ppermute(value, "aa", [(i, i ^ 1) for i in range(8)])


def per_device(spec_in, legendre, pair_wave, quad_weight, forcing):
    me = lax.axis_index("aa").astype(jnp.int32).reshape(1)
    legendre = pltpu.with_memory_space_constraint(legendre, pltpu.HBM)
    wave_table = pltpu.with_memory_space_constraint(pair_wave, pltpu.HBM)
    spec = jnp.swapaxes(spec_in.reshape(PAIRS, 2, FIELDS, -1), 1, 2)
    spec = pltpu.with_memory_space_constraint(spec, pltpu.HBM)
    forcing_send, spec = pack_rows(forcing.reshape(24, OWNERS, COLS), spec)
    forcing_here = lax.all_to_all(forcing_send, "ba", split_axis=0, concat_axis=0, tiled=True)
    fourier = legendre_inverse(wave_table, me, legendre, spec)
    pairs = pair_wave.astype(F32).reshape(8, PAIRS)
    waves = jnp.pad(jnp.stack([pairs, TRUNCATION - pairs], axis=1), ((0, 0), (0, 0), (0, 48)))
    waves, forcing_here = lax.optimization_barrier((waves, forcing_here))
    outer, inner, factor = phase_tables(me, waves)
    came = [fourier[0]] + [to_chip(fourier[s], s) for s in range(1, 4)]
    *came, factor = lax.optimization_barrier((*came, factor))
    kept = jnp.stack([c[0] for c in came])
    got = to_other_core(jnp.stack([c[1] for c in came]))
    grid_send, own, other, block = transform_rows(
        me, quad_weight, kept, got, forcing_here, outer, inner, factor, legendre
    )
    staying, grid_send = lax.optimization_barrier((own[0], grid_send))
    grid_came = lax.all_to_all(grid_send, "ba", split_axis=0, concat_axis=0, tiled=True)
    passed = to_other_core(other)
    parts = [jnp.stack([own[s] if s else staying, passed[s]]) for s in range(4)]
    came = [parts[0]] + [to_chip(parts[s], -s) for s in range(1, 4)]
    spec_out = legendre_direct(wave_table, me, came, legendre, block)
    grid = unpack_rows(grid_came)
    return (
        grid.reshape(8, FIELDS, OWNERS, COLS),
        jnp.swapaxes(spec_out, 1, 2).reshape(PAIRS, 2, FIELDS, 1, -1),
    )


def solution(mesh):
    placed = (
        P("aa", None, None, "ba", None),
        P("aa", None, None),
        P(),
        P(),
        P("aa", None, None, "ba"),
    )
    return jax.shard_map(
        per_device,
        mesh=mesh,
        in_specs=placed,
        out_specs=(P("aa", None, None, "ba"), P("aa", None, None, "ba", None)),
        check_vma=False,
    )
```
